128 devices in a mesh: gx: 8 (over z, core), gy: 4 (over y), gz: 4 (over x).
Axes of the slice: x: 4, y: 4, z: 4, core: 2. Of those that a mesh axis runs over, the one named last changes fastest.
Arguments:
- orbitals: bfloat16 [2, 512, 64000], P(None, ('gx', 'gy', 'gz')), may hold values from -6 to 6
- dest: int32 [512], replicated, may hold values from 0 to 127, as said below
- partners: int32 [512, 2], replicated, may hold values from 0 to 511, as said below
- anchors: int32 [512, 3], replicated, may hold values from 0 to 767, as said below
Outputs:
- exchange: float32 [2, 896, 64000], P(None, ('gx', 'gy', 'gz'))
The draws below stay inside these ranges and needn't reach their ends.
Inputs may be any that keep to these rules, and one draw needn't show every extreme that they name: `dest`: box i goes to its first device or to the device just before or just after it in the numbering; a device passes at most 2 boxes to the device before and at most 1 to the device after, and holds at most 7 boxes after the move; every device holds one or more; each of these three bounds is reached in every draw. A box's partners (the box itself or the same box twice may occur) sit at first on the same device as the box or on one next to it in the numbering, and after the move likewise. Before the move and after it, exactly 1 of the boxes of a device are partners of boxes on the device after it, and exactly 1 are partners of boxes on the device before it (where that device exists). `anchors`: columns are the three grid dimensions, each within its own grid extent; along each, a partner's anchor differs from its box's by at most 20 cells, the difference taken modulo the grid.
All inputs are finite; a program needn't handle non-finite values.
Results may differ from the reference program's by a relative error of at most 0.0072.
Values may be sent and summed in bfloat16 or wider, within the bound.
A program may use at most 64 MiB of HBM per device.

```python
import jax
import jax.numpy as jnp
from jax import lax

SPINS = 2
EDGE = 40
CELLS = 64000
PARTNERS = 2
GRID_X = 768
GRID_Y = 384
GRID_Z = 384
BOX_DEV = 4
BACK = 2
AHEAD = 1
CAP = 7
WINDOW = 1
STEP = 10
BOXES = 512
SLOTS = 896
DEVICES = 128


def chain_layout(key):
    devices = BOXES // BOX_DEV
    subkeys = [jax.random.fold_in(key, 101 + number) for number in range(9)]
    ahead_count = jax.random.randint(subkeys[0], (devices + 1,), 1, AHEAD + 1)
    back_count = jax.random.randint(subkeys[1], (devices + 1,), 1, BACK + 1)
    marker = jax.random.randint(subkeys[2], (), 2, devices - 2)
    bound_index = jnp.arange(devices + 1)
    ahead_count = jnp.where(bound_index == marker, AHEAD, ahead_count)
    ahead_count = jnp.where(bound_index == marker + 1, 0, ahead_count)
    back_count = jnp.where(bound_index == marker, 0, back_count)
    back_count = jnp.where(bound_index == marker + 1, BACK, back_count)
    at_ends = (bound_index == 0) | (bound_index == devices)
    ahead_count = jnp.where(at_ends, 0, ahead_count).astype(jnp.int32)
    back_count = jnp.where(at_ends, 0, back_count).astype(jnp.int32)
    box_ids = jnp.arange(BOXES, dtype=jnp.int32)
    owner = box_ids // BOX_DEV
    shuffles = jax.vmap(lambda subkey: jax.random.permutation(subkey, BOX_DEV))(jax.random.split(subkeys[3], devices))
    rank = shuffles.reshape(-1).astype(jnp.int32)
    box_of = jnp.zeros((BOXES,), jnp.int32).at[owner * BOX_DEV + rank].set(box_ids)
    back_own = jnp.take(back_count, owner)
    ahead_next = jnp.take(ahead_count, owner + 1)
    go_back = rank < back_own
    go_ahead = rank >= BOX_DEV - ahead_next
    dest = (owner - go_back.astype(jnp.int32) + go_ahead.astype(jnp.int32)).astype(jnp.int32)
    core_count = BOX_DEV - back_own - ahead_next
    random_pick = jax.random.randint(subkeys[4], (BOXES,), 0, WINDOW)
    core_pick = (rank - back_own) % WINDOW
    picked = jnp.where(go_back | go_ahead, random_pick, core_pick)
    own_rank = back_own + jax.random.randint(subkeys[5], (BOXES,), 0, BOX_DEV) % core_count
    own_core = jnp.take(box_of, owner * BOX_DEV + own_rank)
    first_dev = jnp.where(go_ahead, owner, owner - 1)
    first_safe = jnp.clip(first_dev, 0, devices - 1)
    plus_box = jnp.take(box_of, first_safe * BOX_DEV + jnp.take(back_count, first_safe) + picked)
    first = jnp.where(first_dev < 0, own_core, plus_box)
    second_dev = jnp.where(go_back, owner, owner + 1)
    second_safe = jnp.clip(second_dev, 0, devices - 1)
    minus_box = jnp.take(box_of, second_safe * BOX_DEV + BOX_DEV - jnp.take(ahead_count, second_safe + 1) - 1 - picked)
    second = jnp.where(second_dev > devices - 1, own_core, minus_box)
    partners = jnp.stack([first, second], axis=1).astype(jnp.int32)
    strides = jax.random.randint(subkeys[6], (devices, 3), -STEP, STEP + 1)
    opening = jax.random.randint(subkeys[7], (1, 3), 0, GRID_Y)
    base = opening + jnp.cumsum(strides, axis=0)
    jitter = jax.random.randint(subkeys[8], (BOXES, 3), 0, STEP + 1)
    extent = jnp.array([GRID_X, GRID_Y, GRID_Z], jnp.int32)
    anchors = ((jnp.take(base, owner, axis=0) + jitter) % extent).astype(jnp.int32)
    lift = GRID_X - 1 - jnp.max(anchors[:, 0])
    anchors = anchors.at[:, 0].add(lift).astype(jnp.int32)
    return (dest, partners, anchors)


def draw_dest(key, part):
    return chain_layout(key)[0]


def draw_partners(key, part):
    return chain_layout(key)[1]


def draw_anchors(key, part):
    return chain_layout(key)[2]


def level_of(rng, dims, cuts, low, largest):
    gain, own = 1.0, jax.random.fold_in(rng, 6)
    for dim, parts in cuts:
        heights = jnp.exp(jax.random.uniform(jax.random.fold_in(own, dim), (parts,), jnp.float32, low / len(cuts), largest / len(cuts)))
        gain = gain * jnp.repeat(heights, dims[dim] // parts).reshape([-1 if axis == dim else 1 for axis in range(len(dims))])
    return gain


def gaussian(key, shape, spread, limit, pieces=(), held_as=jnp.bfloat16):
    result = jax.random.normal(key, shape, jnp.float32) * spread
    if len(pieces) > 0:
        result = level_of(key, shape, pieces, -0.22, 0.18) * result
    return jnp.clip(result, min=-limit, max=limit).astype(held_as)


def setup_inputs(seed: int = 0) -> dict:
    keys = jax.random.split(jax.random.key(seed), 5)
    return {
        "orbitals": gaussian(keys[0], (SPINS, BOXES, CELLS), 1.0, 6.0, ((1, 128),)),
        "dest": draw_dest(jax.random.fold_in(keys[4], 71), 0),
        "partners": draw_partners(jax.random.fold_in(keys[4], 71), 0),
        "anchors": draw_anchors(jax.random.fold_in(keys[4], 71), 0),
    }


SCREEN = 0.001

def sine_basis(edge_cells):
    counter = jnp.arange(edge_cells, dtype=jnp.float32) + 1.0
    angles = jnp.pi * counter[:, None] * counter[None, :] / (edge_cells + 1.0)
    sine_table = (jnp.sqrt(2.0 / (edge_cells + 1.0)) * jnp.sin(angles)).astype(jnp.bfloat16)
    levels = 2.0 - 2.0 * jnp.cos(jnp.pi * counter / (edge_cells + 1.0))
    spectrum = levels[:, None, None] + levels[None, :, None] + levels[None, None, :] + SCREEN
    return (sine_table, spectrum)

def sine_pass(volume, sine_table):
    finest = lax.Precision.HIGHEST
    table = sine_table.astype(jnp.float32)
    volume = jnp.einsum('ak,sabc->skbc', table, volume.astype(jnp.float32), precision=finest).astype(jnp.bfloat16)
    volume = jnp.einsum('bk,sabc->sakc', table, volume.astype(jnp.float32), precision=finest).astype(jnp.bfloat16)
    return jnp.einsum('ck,sabc->sabk', table, volume.astype(jnp.float32), precision=finest)

def reference(orbitals, dest, partners, anchors):
    sine_table, spectrum = sine_basis(EDGE)
    extent = jnp.array([GRID_X, GRID_Y, GRID_Z], dtype=jnp.int32)
    cube_shape = (SPINS, EDGE, EDGE, EDGE)

    def box_term(box_index):
        center = orbitals[:, box_index].astype(jnp.float32).reshape(cube_shape)
        summed = jnp.zeros(cube_shape, jnp.float32)
        for number in range(PARTNERS):
            partner_id = partners[box_index, number]
            difference = anchors[partner_id] - anchors[box_index]
            shift_by = jnp.clip((difference + extent // 2) % extent - extent // 2, -EDGE, EDGE)
            partner_cube = orbitals[:, partner_id].astype(jnp.float32).reshape(cube_shape)
            padded = jnp.pad(partner_cube, ((0, 0), (EDGE, EDGE), (EDGE, EDGE), (EDGE, EDGE)))
            corner = (EDGE - shift_by).astype(jnp.int32)
            shifted = lax.dynamic_slice(padded, (jnp.int32(0), corner[0], corner[1], corner[2]), cube_shape)
            density = (center * shifted).astype(jnp.bfloat16)
            spectral = (sine_pass(density, sine_table) / spectrum).astype(jnp.bfloat16)
            potential = sine_pass(spectral, sine_table)
            summed = summed + potential * shifted
        return summed.reshape(SPINS, CELLS)
    box_terms = lax.map(box_term, jnp.arange(BOXES, dtype=jnp.int32))
    onehot = (dest[:, None] == jnp.arange(DEVICES, dtype=jnp.int32)[None, :]).astype(jnp.int32)
    before_count = jnp.cumsum(onehot, axis=0) - onehot
    slot_of = dest * CAP + lax.optimization_barrier(jnp.sum(before_count * onehot, axis=1))
    exchange = jnp.zeros((SPINS, SLOTS, CELLS), jnp.float32)
    return exchange.at[:, slot_of].set(jnp.moveaxis(box_terms, 0, 1))
```

```python
import functools

import jax
import jax.numpy as jnp
import ml_dtypes
import numpy as np
from jax import lax
from jax.experimental import pallas as pl
from jax.experimental.pallas import tpu as pltpu
from jax.sharding import PartitionSpec as P

AXES = ("gx", "gy", "gz")
DEVICES = 128
SPINS = 2
EDGE = 40
PLANE = EDGE * EDGE
CELLS = EDGE * PLANE
GRID = (768, 384, 384)
BOX_DEV = 4
CAP = 7
SCREEN = 0.001

LANE = 128
TILES = 13
WIDTH = TILES * LANE
OFF = (WIDTH - PLANE) // 2
MARGIN = 7 * LANE
WIDE = WIDTH + 2 * MARGIN
ROWS = SPINS * EDGE
TOP = 24
PAIR_ROWS = BOX_DEV * 2 * ROWS


def tables():
    counter = np.arange(EDGE, dtype=np.float64) + 1.0
    angles = np.pi * counter[:, None] * counter[None, :] / (EDGE + 1.0)
    sine = (np.sqrt(2.0 / (EDGE + 1.0)) * np.sin(angles)).astype(ml_dtypes.bfloat16)
    levels = 2.0 - 2.0 * np.cos(np.pi * counter / (EDGE + 1.0))
    plane = (levels[:, None] + levels[None, :]).reshape(-1)
    inverse = np.zeros((EDGE, WIDTH), np.float32)
    inverse[:, OFF : OFF + PLANE] = 1.0 / (levels[:, None] + plane[None, :] + SCREEN)
    inverse = np.concatenate([inverse, inverse], axis=0)
    sine32 = sine.astype(np.float32)
    first = np.kron(np.eye(4, dtype=np.float32), sine32).astype(ml_dtypes.bfloat16)
    both = np.zeros((WIDTH, WIDTH), np.float32)
    both[OFF : OFF + PLANE, OFF : OFF + PLANE] = np.kron(sine32, sine32)
    both = both.astype(ml_dtypes.bfloat16)
    cells = np.full((2, WIDTH), -1000, np.int32)
    cells[0, OFF : OFF + PLANE] = np.arange(PLANE) // EDGE
    cells[1, OFF : OFF + PLANE] = np.arange(PLANE) % EDGE
    return first, both, inverse, cells


def device_number():
    index = lax.axis_index(AXES[0])
    for name in AXES[1:]:
        index = index * lax.axis_size(name) + lax.axis_index(name)
    return index


def count(dest, first_box, device):
    total = 0
    for number in range(BOX_DEV):
        total = total + (dest[first_box + number] == device).astype(jnp.int32)
    return total


def position(backs, aheads, rank):
    place = backs + rank
    return place + jnp.where((place >= 2) & (aheads > 0), 1, 0)


def boxes_by_position(dest, device):
    base = device * BOX_DEV
    backs = count(dest, base, device - 1)
    aheads = count(dest, base, device + 1)
    order = [0] * BOX_DEV
    back_rank = stay_rank = 0
    for number in range(BOX_DEV):
        goal = dest[base + number]
        back = goal < device
        ahead = goal > device
        place = jnp.where(back, back_rank, jnp.where(ahead, 2, position(backs, aheads, stay_rank)))
        back_rank = back_rank + back.astype(jnp.int32)
        stay_rank = stay_rank + (goal == device).astype(jnp.int32)
        for spot in range(BOX_DEV):
            order[spot] = order[spot] + jnp.where(place == spot, number, 0)
    return order


def slot_sources(dest, device):
    base = device * BOX_DEV
    last = DEVICES - 1
    backs = count(dest, base, device - 1)
    aheads = count(dest, base, device + 1)
    stays = BOX_DEV - backs - aheads
    behind = jnp.maximum(device - 1, 0) * BOX_DEV
    front = jnp.minimum(device + 1, last) * BOX_DEV
    from_prev = jnp.where(device > 0, count(dest, behind, device), 0)
    from_next = jnp.where(device < last, count(dest, front, device), 0)
    sources = []
    for slot in range(CAP):
        rank = slot - from_prev
        late = rank - stays
        sources.append(
            jnp.where(
                rank < 0,
                4,
                jnp.where(
                    late < 0,
                    position(backs, aheads, rank),
                    jnp.where(late < from_next, 5 + late, 7),
                ),
            )
        )
    return sources


def shared_box(partners, device, other):
    inside = jnp.clip(other, 0, DEVICES - 1) * BOX_DEV
    chosen = 0
    for number in range(BOX_DEV):
        for which in range(2):
            partner = partners[which, inside + number] - device * BOX_DEV
            chosen = jnp.where((partner >= 0) & (partner < BOX_DEV), partner, chosen)
    return chosen


def wrapped(difference, extent):
    half = difference + extent // 2
    half = jnp.where(half < 0, half + extent, half)
    half = jnp.where(half >= extent, half - extent, half)
    return half - extent // 2


def unpack_rows(orbitals, store):
    def pair(number, carry):
        start = pl.multiple_of(number * 2 * PLANE, LANE)
        for spin in range(SPINS):
            cells = orbitals[spin, :, pl.ds(start, 2 * PLANE)].astype(jnp.float32)
            even = pltpu.roll(cells[:, :WIDTH], OFF, 1)
            odd = pltpu.roll(cells[:, 2 * PLANE - WIDTH :], WIDTH - OFF, 1)
            store(spin * EDGE + 2 * number, even)
            store(spin * EDGE + 2 * number + 1, odd)
        return carry

    lax.fori_loop(0, EDGE // 2, pair, 0)


def shift_pair(boxes, moved, density, cells, center_row, partner_row, delta, pair_row):
    flat = MARGIN - (delta[1] * EDGE + delta[2])
    column = flat // LANE
    turn = flat - column * LANE
    center_row = pl.multiple_of(center_row, 8)
    lanes = lax.broadcasted_iota(jnp.int32, (EDGE, LANE), 1)
    keep = lanes < LANE - turn
    rows = lax.broadcasted_iota(jnp.int32, (EDGE, LANE), 0) - delta[0]
    row_ok = (rows >= 0) & (rows < EDGE)

    def load(tile, spin):
        value = boxes[column + tile, pl.ds(partner_row + spin * EDGE - delta[0], EDGE), :]
        return pltpu.roll(value, LANE - turn, 1)

    before = [load(0, spin) for spin in range(SPINS)]
    for tile in range(TILES):
        span = slice(tile * LANE, (tile + 1) * LANE)
        second = cells[0:1, span] - delta[1]
        third = cells[1:2, span] - delta[2]
        inside = (second >= 0) & (second < EDGE) & (third >= 0) & (third < EDGE)
        inside = inside & (cells[0:1, span] >= 0)
        ok = row_ok & inside
        after = [load(tile + 1, spin) for spin in range(SPINS)]
        values = []
        products = []
        for spin in range(SPINS):
            value = jnp.where(ok, jnp.where(keep, before[spin], after[spin]), 0.0)
            center = boxes[MARGIN // LANE + tile, pl.ds(center_row + spin * EDGE, EDGE), :]
            values.append(value)
            products.append(center * value)
        before = after
        target = pl.ds(pl.multiple_of(pair_row, ROWS), ROWS)
        moved[target, span] = jnp.concatenate(values, axis=0)
        density[target, span] = jnp.concatenate(products, axis=0).astype(jnp.bfloat16)


CHUNKS = [(start, min(256, WIDTH - start)) for start in range(0, WIDTH, 256)]


def solve(density, work, first, both, inverse):
    rows = density.shape[0]
    for block in range(rows // (2 * ROWS)):
        span = slice(block * 2 * ROWS, (block + 1) * 2 * ROWS)
        work[span, :] = jnp.dot(
            first[...], density[span, :], preferred_element_type=jnp.float32
        ).astype(jnp.bfloat16)
    for start, size in CHUNKS:
        scale = inverse[:, start : start + size]
        out = jnp.dot(work[...], both[:, start : start + size], preferred_element_type=jnp.float32)
        out = out.reshape(rows // ROWS, ROWS, size) * scale[None]
        density[:, start : start + size] = out.reshape(rows, size).astype(jnp.bfloat16)
    for start, size in CHUNKS:
        work[:, start : start + size] = jnp.dot(
            density[...], both[:, start : start + size], preferred_element_type=jnp.float32
        ).astype(jnp.bfloat16)


def pack_kernel(dest, partners, orbitals, rows, to_next, to_prev, scratch):
    device = device_number()

    def store(row, value):
        for tile in range(TILES):
            scratch[tile, pl.ds(row, BOX_DEV, stride=ROWS), :] = value[:, tile * LANE : (tile + 1) * LANE]

    unpack_rows(orbitals, store)
    rows[...] = scratch[...].astype(jnp.bfloat16)
    ahead = shared_box(partners, device, device + 1)
    back = shared_box(partners, device, device - 1)
    to_next[...] = scratch[:, pl.ds(pl.multiple_of(ahead * ROWS, 8), ROWS), :].astype(jnp.bfloat16)
    to_prev[...] = scratch[:, pl.ds(pl.multiple_of(back * ROWS, 8), ROWS), :].astype(jnp.bfloat16)


def solve_kernel(
    dest, partners, anchors, rows, prev_box, next_box, first, both, inverse, cells,
    results, sends, boxes, moved, density, work,
):
    device = device_number()
    own = BOX_DEV * ROWS
    middle = slice(MARGIN // LANE, MARGIN // LANE + TILES)
    boxes[middle, TOP : TOP + own, :] = rows[...].astype(jnp.float32)
    boxes[middle, TOP + own : TOP + own + ROWS, :] = prev_box[...].astype(jnp.float32)
    boxes[middle, TOP + own + ROWS : TOP + own + 2 * ROWS, :] = next_box[...].astype(jnp.float32)
    order = boxes_by_position(dest, device)
    base = device * BOX_DEV
    for spot in range(BOX_DEV):
        box = base + order[spot]
        for which in range(2):
            partner = partners[which, box]
            local = partner - base
            place = jnp.where(local < 0, 4, jnp.where(local >= BOX_DEV, 5, local))
            delta = [
                wrapped(anchors[dim, partner] - anchors[dim, box], GRID[dim]) for dim in range(3)
            ]
            shift_pair(
                boxes, moved, density, cells, TOP + order[spot] * ROWS, TOP + place * ROWS, delta,
                (spot * 2 + which) * ROWS,
            )
    solve(density, work, first, both, inverse)
    for spot in range(BOX_DEV):
        span = slice(spot * 2 * ROWS, (spot + 1) * 2 * ROWS)
        potential = jnp.dot(first[...], work[span, :], preferred_element_type=jnp.float32)
        terms = potential * moved[span, :]
        total = terms[:ROWS] + terms[ROWS:]
        for tile in range(TILES):
            part = total[:, tile * LANE : (tile + 1) * LANE]
            results[tile, spot * ROWS : (spot + 1) * ROWS, :] = part
            if spot < 3:
                sends[spot, tile, :, :] = part.astype(jnp.bfloat16)


def assemble_kernel(dest, results, prev_results, next_results, out, scratch):
    device = device_number()
    slot = pl.program_id(0)

    @pl.when(slot == 0)
    def _():
        scratch[:, : 4 * ROWS, :] = results[...]
        scratch[:, 4 * ROWS : 5 * ROWS, :] = prev_results[0].astype(jnp.float32)
        scratch[:, 5 * ROWS : 6 * ROWS, :] = next_results[0].astype(jnp.float32)
        scratch[:, 6 * ROWS : 7 * ROWS, :] = next_results[1].astype(jnp.float32)
        scratch[:, 7 * ROWS :, :] = jnp.zeros((TILES, ROWS, LANE), jnp.float32)

    sources = slot_sources(dest, device)
    source = sources[0]
    for number in range(1, CAP):
        source = jnp.where(slot == number, sources[number], source)
    lanes = lax.broadcasted_iota(jnp.int32, (SPINS, LANE), 1)

    def line(row):
        pieces = [scratch[tile, pl.ds(row, SPINS, stride=EDGE), :] for tile in range(TILES)]
        return jnp.concatenate(pieces, axis=1)

    def pair(number, carry):
        row = source * ROWS + 2 * number
        even = pltpu.roll(line(row), WIDTH - OFF, 1)
        odd = pltpu.roll(line(row + 1), OFF, 1)
        middle = jnp.where(lanes < LANE // 2, even[:, WIDTH - LANE :], odd[:, :LANE])
        start = pl.multiple_of(number * 2 * PLANE, LANE)
        cells = jnp.concatenate([even[:, : WIDTH - LANE], middle, odd[:, LANE:]], axis=1)
        out[0, :, pl.ds(start, 2 * PLANE)] = cells
        return carry

    lax.fori_loop(0, EDGE // 2, pair, 0)


VMEM_LIMIT = 56 * 1024 * 1024


def shards(orbitals, dest, partners, anchors):
    first, both, inverse, cells = (jnp.asarray(table) for table in tables())
    partners = partners.T
    anchors = anchors.T
    smem = pl.BlockSpec(memory_space=pltpu.SMEM)
    vmem = pl.BlockSpec(memory_space=pltpu.VMEM)
    params = pltpu.CompilerParams(vmem_limit_bytes=VMEM_LIMIT)
    own = BOX_DEV * ROWS
    box_shape = jax.ShapeDtypeStruct((TILES, ROWS, LANE), jnp.bfloat16)
    rows, to_next, to_prev = pl.pallas_call(
        pack_kernel,
        out_shape=(jax.ShapeDtypeStruct((TILES, own, LANE), jnp.bfloat16), box_shape, box_shape),
        in_specs=[smem, smem, vmem],
        out_specs=[vmem] * 3,
        scratch_shapes=[pltpu.VMEM((TILES, own, LANE), jnp.float32)],
        compiler_params=params,
    )(dest, partners, orbitals)
    ahead = [(number, number + 1) for number in range(DEVICES - 1)]
    back = [(number + 1, number) for number in range(DEVICES - 1)]
    prev_box = lax.ppermute(to_next, AXES, ahead)
    next_box = lax.ppermute(to_prev, AXES, back)
    results, sends = pl.pallas_call(
        solve_kernel,
        out_shape=(
            jax.ShapeDtypeStruct((TILES, own, LANE), jnp.float32),
            jax.ShapeDtypeStruct((3, TILES, ROWS, LANE), jnp.bfloat16),
        ),
        in_specs=[smem] * 3 + [vmem] * 7,
        out_specs=[vmem] * 2,
        scratch_shapes=[
            pltpu.VMEM((WIDE // LANE, TOP + 6 * ROWS + TOP, LANE), jnp.float32),
            pltpu.VMEM((PAIR_ROWS, WIDTH), jnp.float32),
            pltpu.VMEM((PAIR_ROWS, WIDTH), jnp.bfloat16),
            pltpu.VMEM((PAIR_ROWS, WIDTH), jnp.bfloat16),
        ],
        compiler_params=params,
    )(dest, partners, anchors, rows, prev_box, next_box, first, both, inverse, cells)
    prev_results = lax.ppermute(sends[2:], AXES, ahead)
    next_results = lax.ppermute(sends[:2], AXES, back)
    out = pl.pallas_call(
        assemble_kernel,
        out_shape=jax.ShapeDtypeStruct((CAP, SPINS, CELLS), jnp.float32),
        grid=(CAP,),
        in_specs=[smem, vmem, vmem, vmem],
        out_specs=pl.BlockSpec((1, SPINS, CELLS), lambda slot: (slot, 0, 0)),
        scratch_shapes=[pltpu.VMEM((TILES, 8 * ROWS, LANE), jnp.float32)],
        compiler_params=params,
    )(dest, results, prev_results, next_results)
    return jnp.transpose(out, (1, 0, 2))


def solution(mesh):
    return jax.shard_map(
        shards,
        mesh=mesh,
        in_specs=(P(None, AXES, None), P(), P(), P()),
        out_specs=P(None, AXES, None),
        check_vma=False,
    )
```

```python
import functools

import jax
import jax.numpy as jnp
import ml_dtypes
import numpy as np
from jax import lax
from jax.experimental import pallas as pl
from jax.experimental.pallas import tpu as pltpu
from jax.sharding import PartitionSpec as P

AXES = ("gx", "gy", "gz")
DEVICES = 128
SPINS = 2
EDGE = 40
PLANE = EDGE * EDGE
CELLS = EDGE * PLANE
GRID = (768, 384, 384)
BOX_DEV = 4
CAP = 7
SCREEN = 0.001

LANE = 128
TILES = 13
WIDTH = TILES * LANE
OFF = (WIDTH - PLANE) // 2
MARGIN = 7 * LANE
WIDE = WIDTH + 2 * MARGIN
ROWS = SPINS * EDGE
PAIR_ROWS = BOX_DEV * 2 * ROWS
OUT_ROWS = SPINS * CELLS // LANE
BATCHES = ((0, 1), (1, 2), (3, 1))
GROUP = 25
EMPTY = MARGIN // LANE
SPREAD = WIDE // LANE
MESH = pl.DeviceIdType.MESH


def tables():
    counter = np.arange(EDGE, dtype=np.float64) + 1.0
    angles = np.pi * counter[:, None] * counter[None, :] / (EDGE + 1.0)
    sine = (np.sqrt(2.0 / (EDGE + 1.0)) * np.sin(angles)).astype(ml_dtypes.bfloat16)
    levels = 2.0 - 2.0 * np.cos(np.pi * counter / (EDGE + 1.0))
    plane = (levels[:, None] + levels[None, :]).reshape(-1)
    inverse = np.zeros((EDGE, WIDTH), np.float32)
    inverse[:, OFF : OFF + PLANE] = 1.0 / (levels[:, None] + plane[None, :] + SCREEN)
    inverse = np.concatenate([inverse, inverse], axis=0)
    sine32 = sine.astype(np.float32)
    first = np.kron(np.eye(4, dtype=np.float32), sine32).astype(ml_dtypes.bfloat16)
    both = np.zeros((WIDTH, WIDTH), np.float32)
    both[OFF : OFF + PLANE, OFF : OFF + PLANE] = np.kron(sine32, sine32)
    both = both.astype(ml_dtypes.bfloat16)
    cells = np.full((2, WIDTH), -1000, np.int32)
    cells[0, OFF : OFF + PLANE] = np.arange(PLANE) // EDGE
    cells[1, OFF : OFF + PLANE] = np.arange(PLANE) % EDGE
    return first, both, inverse, cells


def device_number():
    index = lax.axis_index(AXES[0])
    for name in AXES[1:]:
        index = index * lax.axis_size(name) + lax.axis_index(name)
    return index


def count(dest, first_box, device):
    total = 0
    for number in range(BOX_DEV):
        total = total + (dest[first_box + number] == device).astype(jnp.int32)
    return total


def position(backs, aheads, rank):
    place = backs + rank
    return place + jnp.where((place >= 2) & (aheads > 0), 1, 0)


def boxes_by_position(dest, device):
    base = device * BOX_DEV
    backs = count(dest, base, device - 1)
    aheads = count(dest, base, device + 1)
    order = [0] * BOX_DEV
    back_rank = stay_rank = 0
    for number in range(BOX_DEV):
        goal = dest[base + number]
        back = goal < device
        ahead = goal > device
        place = jnp.where(back, back_rank, jnp.where(ahead, 2, position(backs, aheads, stay_rank)))
        back_rank = back_rank + back.astype(jnp.int32)
        stay_rank = stay_rank + (goal == device).astype(jnp.int32)
        for spot in range(BOX_DEV):
            order[spot] = order[spot] + jnp.where(place == spot, number, 0)
    return order


def slot_sources(dest, device):
    base = device * BOX_DEV
    last = DEVICES - 1
    backs = count(dest, base, device - 1)
    aheads = count(dest, base, device + 1)
    stays = BOX_DEV - backs - aheads
    behind = jnp.maximum(device - 1, 0) * BOX_DEV
    front = jnp.minimum(device + 1, last) * BOX_DEV
    from_prev = jnp.where(device > 0, count(dest, behind, device), 0)
    from_next = jnp.where(device < last, count(dest, front, device), 0)
    sources = []
    for slot in range(CAP):
        rank = slot - from_prev
        late = rank - stays
        sources.append(
            jnp.where(
                rank < 0,
                4,
                jnp.where(
                    late < 0,
                    position(backs, aheads, rank),
                    jnp.where(late < from_next, 5 + late, 7),
                ),
            )
        )
    return sources


def shared_box(partners, device, other):
    inside = jnp.clip(other, 0, DEVICES - 1) * BOX_DEV
    chosen = 0
    for number in range(BOX_DEV):
        for which in range(2):
            partner = partners[which, inside + number] - device * BOX_DEV
            chosen = jnp.where((partner >= 0) & (partner < BOX_DEV), partner, chosen)
    return chosen


def wrapped(difference, extent):
    half = difference + extent // 2
    half = jnp.where(half < 0, half + extent, half)
    half = jnp.where(half >= extent, half - extent, half)
    return half - extent // 2


def pick(values, index):
    chosen = values[0]
    for number in range(1, len(values)):
        chosen = jnp.where(index == number, values[number], chosen)
    return chosen


def unpack_rows(orbitals, lines, boxes):
    def pair(number, carry):
        start = pl.multiple_of(number * 2 * PLANE, LANE)
        for spin in range(SPINS):
            cells = orbitals[spin, :, pl.ds(start, 2 * PLANE)].astype(jnp.float32)
            even = pltpu.roll(cells[:, :WIDTH], OFF, 1)
            odd = pltpu.roll(cells[:, 2 * PLANE - WIDTH :], WIDTH - OFF, 1)
            row = spin * EDGE + 2 * number
            for tile in range(TILES):
                span = slice(tile * LANE, (tile + 1) * LANE)
                lines[tile, pl.ds(row, BOX_DEV, stride=ROWS), :] = even[:, span]
                lines[tile, pl.ds(row + 1, BOX_DEV, stride=ROWS), :] = odd[:, span]
        return carry

    lax.fori_loop(0, EDGE // 2, pair, 0)
    for box in range(BOX_DEV):
        for tile in range(TILES):
            value = lines[tile, box * ROWS : (box + 1) * ROWS, :]
            boxes[box * SPREAD + EMPTY + tile] = value.astype(jnp.bfloat16)


def shift_pair(boxes, moved, density, cells, center, partner, delta, pair_row):
    flat = MARGIN - (delta[1] * EDGE + delta[2])
    column = flat // LANE
    turn = flat - column * LANE
    pair_row = pl.multiple_of(pair_row, ROWS)
    keep = lax.broadcasted_iota(jnp.int32, (ROWS, LANE), 1) < LANE - turn
    row = lax.broadcasted_iota(jnp.int32, (ROWS, ROWS), 0)
    source = lax.broadcasted_iota(jnp.int32, (ROWS, ROWS), 1)
    same = (row >= EDGE) == (source >= EDGE)
    shifter = (same & (source == row - delta[0])).astype(jnp.float32).astype(jnp.bfloat16)
    first_tile = partner * SPREAD + column
    wide = jnp.concatenate([boxes[first_tile + tile] for tile in range(TILES + 1)], axis=1)
    wide = jnp.dot(shifter, wide, preferred_element_type=jnp.float32)
    turned = [
        pltpu.roll(wide[:, tile * LANE : (tile + 1) * LANE], LANE - turn, 1)
        for tile in range(TILES + 1)
    ]
    for tile in range(TILES):
        span = slice(tile * LANE, (tile + 1) * LANE)
        second = cells[0:1, span] - delta[1]
        third = cells[1:2, span] - delta[2]
        inside = (second >= 0) & (second < EDGE) & (third >= 0) & (third < EDGE)
        inside = inside & (cells[0:1, span] >= 0)
        value = jnp.where(inside, jnp.where(keep, turned[tile], turned[tile + 1]), 0.0)
        product = boxes[center * SPREAD + EMPTY + tile].astype(jnp.float32) * value
        moved[pl.ds(pair_row, ROWS), span] = value
        density[pl.ds(pair_row, ROWS), span] = product.astype(jnp.bfloat16)


def by_chunk(body):
    def step(number, carry):
        body(pl.multiple_of(number * 256, 256), 256)
        return carry

    lax.fori_loop(0, WIDTH // 256, step, 0)
    body(WIDTH // 256 * 256, WIDTH % 256)


def solve(density, work, first, both, inverse, low, rows):
    span = slice(low, low + rows)
    for block in range(rows // (2 * ROWS)):
        part = slice(low + block * 2 * ROWS, low + (block + 1) * 2 * ROWS)
        work[part, :] = jnp.dot(
            first[...], density[part, :], preferred_element_type=jnp.float32
        ).astype(jnp.bfloat16)

    def forward(start, size):
        cut = pl.ds(start, size)
        out = jnp.dot(work[span, :], both[:, cut], preferred_element_type=jnp.float32)
        out = out.reshape(rows // ROWS, ROWS, size) * inverse[:, cut][None]
        density[span, cut] = out.reshape(rows, size).astype(jnp.bfloat16)

    def backward(start, size):
        cut = pl.ds(start, size)
        out = jnp.dot(density[span, :], both[:, cut], preferred_element_type=jnp.float32)
        work[span, cut] = out.astype(jnp.bfloat16)

    by_chunk(forward)
    by_chunk(backward)


def flatten_rows(lines, place):
    half = EDGE // 2
    lanes = lax.broadcasted_iota(jnp.int32, (half, LANE), 1)
    for spin in range(SPINS):
        even = [
            pltpu.roll(lines[tile, pl.ds(spin * EDGE, half, stride=2), :], LANE - OFF, 1)
            for tile in range(TILES)
        ]
        odd = [
            pltpu.roll(lines[tile, pl.ds(spin * EDGE + 1, half, stride=2), :], OFF, 1)
            for tile in range(TILES)
        ]
        for tile in range(TILES - 1):
            place(2 * tile + spin, jnp.where(lanes < LANE - OFF, even[tile], even[tile + 1]))
        place(2 * (TILES - 1) + spin, jnp.where(lanes < LANE // 2, even[TILES - 1], odd[0]))
        for tile in range(1, TILES):
            place(
                2 * (TILES - 1 + tile) + spin,
                jnp.where(lanes < OFF, odd[tile - 1], odd[tile]),
            )


def mesh_place(device):
    gz = lax.axis_size(AXES[2])
    gy = lax.axis_size(AXES[1])
    return (device // (gy * gz), (device // gz) % gy, device % gz)


def solve_kernel(
    dest, partners, anchors, orbitals, first, both_hbm, inverse, cells,
    results, arrived,
    boxes, moved, density, work, both, lines, box_out, box_in, sends,
    table_sem, box_send, box_recv, move_send, move_recv,
):
    device = device_number()
    following = mesh_place((device + 1) % DEVICES)
    previous = mesh_place((device + DEVICES - 1) % DEVICES)
    barrier = pltpu.get_barrier_semaphore()
    for other in (following, previous):
        pl.semaphore_signal(barrier, inc=1, device_id=other, device_id_type=MESH)
    table = pltpu.make_async_copy(both_hbm, both, table_sem)
    table.start()
    blank = jnp.zeros((ROWS, LANE), jnp.bfloat16)
    for box in range(BOX_DEV + 2):
        for tile in range(EMPTY):
            boxes[box * SPREAD + tile] = blank
            boxes[box * SPREAD + EMPTY + TILES + tile] = blank
    unpack_rows(orbitals, lines, boxes)
    box_copies = []
    for way, (other, target) in enumerate(((device + 1, following), (device - 1, previous))):
        chosen = shared_box(partners, device, other)
        for tile in range(TILES):
            box_out[way, tile] = boxes[chosen * SPREAD + EMPTY + tile]
        if way == 0:
            pl.semaphore_wait(barrier, 2)
        copy = pltpu.make_async_remote_copy(
            src_ref=box_out.at[way], dst_ref=box_in.at[way],
            send_sem=box_send.at[way], recv_sem=box_recv.at[way],
            device_id=target, device_id_type=MESH,
        )
        copy.start()
        box_copies.append(copy)
    order = boxes_by_position(dest, device)
    base = device * BOX_DEV
    for way, copy in enumerate(box_copies):
        copy.wait()
        for tile in range(TILES):
            boxes[(BOX_DEV + way) * SPREAD + EMPTY + tile] = box_in[way, tile]

    def pair(number, carry):
        spot = number // 2
        which = number % 2
        local_box = pick(order, spot)
        box = base + local_box
        partner = partners[which, box]
        local = partner - base
        place = jnp.where(local < 0, 4, jnp.where(local >= BOX_DEV, 5, local))
        delta = [wrapped(anchors[dim, partner] - anchors[dim, box], GRID[dim]) for dim in range(3)]
        shift_pair(
            boxes, moved, density, cells, local_box, place, delta, number * ROWS
        )
        return carry

    lax.fori_loop(0, 2 * BOX_DEV, pair, 0)
    table.wait()
    moves = []
    for begin, number in BATCHES:
        solve(density, work, first, both, inverse, begin * 2 * ROWS, number * 2 * ROWS)
        for spot in range(begin, begin + number):
            span = slice(spot * 2 * ROWS, (spot + 1) * 2 * ROWS)
            potential = jnp.dot(first[...], work[span, :], preferred_element_type=jnp.float32)
            terms = potential * moved[span, :]
            total = terms[:ROWS] + terms[ROWS:]
            for tile in range(TILES):
                lines[tile, :ROWS, :] = total[:, tile * LANE : (tile + 1) * LANE]

            def place(row, value):
                results[spot, pl.ds(row, EDGE // 2, stride=2 * (2 * TILES - 1)), :] = value

            flatten_rows(lines, place)
            if spot < 3:
                sends[spot] = results[spot].astype(jnp.bfloat16)
                copy = pltpu.make_async_remote_copy(
                    src_ref=sends.at[spot], dst_ref=arrived.at[spot],
                    send_sem=move_send.at[spot], recv_sem=move_recv.at[spot],
                    device_id=previous if spot < 2 else following, device_id_type=MESH,
                )
                copy.start()
                moves.append(copy)
    for copy in moves:
        copy.wait()


def assemble_kernel(dest, results, arrived, out, wide):
    device = device_number()
    slot = pl.program_id(0)
    source = pick(slot_sources(dest, device), slot)

    @pl.when(slot == 0)
    def _():
        wide[...] = arrived[...].astype(jnp.float32)

    def copy(source_ref):
        def group(number, carry):
            row = number * 2 * GROUP
            column = number * GROUP * LANE
            for tile in range(GROUP):
                start = pl.multiple_of(column + tile * LANE, LANE)
                out[0, :, pl.ds(start, LANE)] = source_ref[pl.ds(row + 2 * tile, SPINS), :]
            return carry

        lax.fori_loop(0, CELLS // (GROUP * LANE), group, 0)

    @pl.when(source < BOX_DEV)
    def _():
        copy(results.at[jnp.minimum(source, BOX_DEV - 1)])

    @pl.when((source >= BOX_DEV) & (source < 7))
    def _():
        copy(wide.at[jnp.where(source == 4, 2, jnp.clip(source - 5, 0, 1))])

    @pl.when(source == 7)
    def _():
        out[...] = jnp.zeros(out.shape, jnp.float32)


VMEM_LIMIT = 56 * 1024 * 1024


def shards(orbitals, dest, partners, anchors):
    first, both, inverse, cells = (jnp.asarray(table) for table in tables())
    partners = partners.T
    anchors = anchors.T
    smem = pl.BlockSpec(memory_space=pltpu.SMEM)
    vmem = pl.BlockSpec(memory_space=pltpu.VMEM)
    hbm = pl.BlockSpec(memory_space=pl.ANY)
    results, arrived = pl.pallas_call(
        solve_kernel,
        out_shape=(
            jax.ShapeDtypeStruct((BOX_DEV, OUT_ROWS, LANE), jnp.float32),
            jax.ShapeDtypeStruct((3, OUT_ROWS, LANE), jnp.bfloat16),
        ),
        in_specs=[smem] * 3 + [vmem, vmem, hbm, vmem, vmem],
        out_specs=[vmem] * 2,
        scratch_shapes=[
            pltpu.VMEM(((BOX_DEV + 2) * SPREAD, ROWS, LANE), jnp.bfloat16),
            pltpu.VMEM((PAIR_ROWS, WIDTH), jnp.float32),
            pltpu.VMEM((PAIR_ROWS, WIDTH), jnp.bfloat16),
            pltpu.VMEM((PAIR_ROWS, WIDTH), jnp.bfloat16),
            pltpu.VMEM((WIDTH, WIDTH), jnp.bfloat16),
            pltpu.VMEM((TILES, BOX_DEV * ROWS, LANE), jnp.float32),
            pltpu.VMEM((2, TILES, ROWS, LANE), jnp.bfloat16),
            pltpu.VMEM((2, TILES, ROWS, LANE), jnp.bfloat16),
            pltpu.VMEM((3, OUT_ROWS, LANE), jnp.bfloat16),
            pltpu.SemaphoreType.DMA,
            pltpu.SemaphoreType.DMA((2,)),
            pltpu.SemaphoreType.DMA((2,)),
            pltpu.SemaphoreType.DMA((3,)),
            pltpu.SemaphoreType.DMA((3,)),
        ],
        compiler_params=pltpu.CompilerParams(
            vmem_limit_bytes=VMEM_LIMIT, collective_id=0, has_side_effects=True
        ),
    )(dest, partners, anchors, orbitals, first, both, inverse, cells)
    out = pl.pallas_call(
        assemble_kernel,
        out_shape=jax.ShapeDtypeStruct((CAP, SPINS, CELLS), jnp.float32),
        grid=(CAP,),
        in_specs=[smem, vmem, vmem],
        out_specs=pl.BlockSpec((1, SPINS, CELLS), lambda slot: (slot, 0, 0)),
        scratch_shapes=[pltpu.VMEM((3, OUT_ROWS, LANE), jnp.float32)],
        compiler_params=pltpu.CompilerParams(vmem_limit_bytes=16 * 1024 * 1024),
    )(dest, results, arrived)
    return jnp.transpose(out, (1, 0, 2))


def solution(mesh):
    return jax.shard_map(
        shards,
        mesh=mesh,
        in_specs=(P(None, AXES, None), P(), P(), P()),
        out_specs=P(None, AXES, None),
        check_vma=False,
    )
```

```python
import functools

import jax
import jax.numpy as jnp
import ml_dtypes
import numpy as np
from jax import lax
from jax.experimental import pallas as pl
from jax.experimental.pallas import tpu as pltpu
from jax.sharding import PartitionSpec as P

AXES = ("gx", "gy", "gz")
DEVICES = 128
SPINS = 2
EDGE = 40
PLANE = EDGE * EDGE
CELLS = EDGE * PLANE
GRID = (768, 384, 384)
BOX_DEV = 4
CAP = 7
SCREEN = 0.001

LANE = 128
TILES = 13
WIDTH = TILES * LANE
OFF = (WIDTH - PLANE) // 2
MARGIN = 7 * LANE
WIDE = WIDTH + 2 * MARGIN
ROWS = SPINS * EDGE
PAIR_ROWS = BOX_DEV * 2 * ROWS
OUT_ROWS = SPINS * CELLS // LANE
GROUP = 25
EMPTY = MARGIN // LANE
SPREAD = WIDE // LANE
MESH = pl.DeviceIdType.MESH


def tables():
    counter = np.arange(EDGE, dtype=np.float64) + 1.0
    angles = np.pi * counter[:, None] * counter[None, :] / (EDGE + 1.0)
    sine = (np.sqrt(2.0 / (EDGE + 1.0)) * np.sin(angles)).astype(ml_dtypes.bfloat16)
    levels = 2.0 - 2.0 * np.cos(np.pi * counter / (EDGE + 1.0))
    plane = (levels[:, None] + levels[None, :]).reshape(-1)
    inverse = np.zeros((EDGE, WIDTH), np.float32)
    inverse[:, OFF : OFF + PLANE] = 1.0 / (levels[:, None] + plane[None, :] + SCREEN)
    inverse = np.concatenate([inverse, inverse], axis=0)
    sine32 = sine.astype(np.float32)
    first = np.kron(np.eye(4, dtype=np.float32), sine32).astype(ml_dtypes.bfloat16)
    both = np.zeros((WIDTH, WIDTH), np.float32)
    both[OFF : OFF + PLANE, OFF : OFF + PLANE] = np.kron(sine32, sine32)
    both = both.astype(ml_dtypes.bfloat16)
    cells = np.full((2, WIDTH), -1000, np.int32)
    cells[0, OFF : OFF + PLANE] = np.arange(PLANE) // EDGE
    cells[1, OFF : OFF + PLANE] = np.arange(PLANE) % EDGE
    return first, both, inverse, cells


def device_number():
    index = lax.axis_index(AXES[0])
    for name in AXES[1:]:
        index = index * lax.axis_size(name) + lax.axis_index(name)
    return index


def count(dest, first_box, device):
    total = 0
    for number in range(BOX_DEV):
        total = total + (dest[first_box + number] == device).astype(jnp.int32)
    return total


def position(backs, aheads, rank):
    place = backs + rank
    return place + jnp.where((place >= 2) & (aheads > 0), 1, 0)


def boxes_by_position(dest, device):
    base = device * BOX_DEV
    backs = count(dest, base, device - 1)
    aheads = count(dest, base, device + 1)
    order = [0] * BOX_DEV
    back_rank = stay_rank = 0
    for number in range(BOX_DEV):
        goal = dest[base + number]
        back = goal < device
        ahead = goal > device
        place = jnp.where(back, back_rank, jnp.where(ahead, 2, position(backs, aheads, stay_rank)))
        back_rank = back_rank + back.astype(jnp.int32)
        stay_rank = stay_rank + (goal == device).astype(jnp.int32)
        for spot in range(BOX_DEV):
            order[spot] = order[spot] + jnp.where(place == spot, number, 0)
    return order


def slot_sources(dest, device):
    base = device * BOX_DEV
    last = DEVICES - 1
    backs = count(dest, base, device - 1)
    aheads = count(dest, base, device + 1)
    stays = BOX_DEV - backs - aheads
    behind = jnp.maximum(device - 1, 0) * BOX_DEV
    front = jnp.minimum(device + 1, last) * BOX_DEV
    from_prev = jnp.where(device > 0, count(dest, behind, device), 0)
    from_next = jnp.where(device < last, count(dest, front, device), 0)
    sources = []
    for slot in range(CAP):
        rank = slot - from_prev
        late = rank - stays
        sources.append(
            jnp.where(
                rank < 0,
                6,
                jnp.where(
                    late < 0,
                    position(backs, aheads, rank),
                    jnp.where(late < from_next, 4 + late, 7),
                ),
            )
        )
    return sources


def shared_box(partners, device, other):
    inside = jnp.clip(other, 0, DEVICES - 1) * BOX_DEV
    chosen = 0
    for number in range(BOX_DEV):
        for which in range(2):
            partner = partners[which, inside + number] - device * BOX_DEV
            chosen = jnp.where((partner >= 0) & (partner < BOX_DEV), partner, chosen)
    return chosen


def wrapped(difference, extent):
    half = difference + extent // 2
    half = jnp.where(half < 0, half + extent, half)
    half = jnp.where(half >= extent, half - extent, half)
    return half - extent // 2


def pick(values, index):
    chosen = values[0]
    for number in range(1, len(values)):
        chosen = jnp.where(index == number, values[number], chosen)
    return chosen


def unpack_rows(orbitals, lines, boxes):
    def pair(number, carry):
        start = pl.multiple_of(number * 2 * PLANE, LANE)
        for spin in range(SPINS):
            cells = orbitals[spin, :, pl.ds(start, 2 * PLANE)].astype(jnp.float32)
            even = pltpu.roll(cells[:, :WIDTH], OFF, 1)
            odd = pltpu.roll(cells[:, 2 * PLANE - WIDTH :], WIDTH - OFF, 1)
            row = spin * EDGE + 2 * number
            for tile in range(TILES):
                span = slice(tile * LANE, (tile + 1) * LANE)
                lines[tile, pl.ds(row, BOX_DEV, stride=ROWS), :] = even[:, span]
                lines[tile, pl.ds(row + 1, BOX_DEV, stride=ROWS), :] = odd[:, span]
        return carry

    lax.fori_loop(0, EDGE // 2, pair, 0)
    for box in range(BOX_DEV):
        for tile in range(TILES):
            value = lines[tile, box * ROWS : (box + 1) * ROWS, :]
            boxes[box * SPREAD + EMPTY + tile] = value.astype(jnp.bfloat16)


def shift_pair(boxes, moved, density, cells, center, partner, delta, pair_row):
    flat = MARGIN - (delta[1] * EDGE + delta[2])
    column = flat // LANE
    turn = flat - column * LANE
    pair_row = pl.multiple_of(pair_row, ROWS)
    keep = lax.broadcasted_iota(jnp.int32, (ROWS, LANE), 1) < LANE - turn
    row = lax.broadcasted_iota(jnp.int32, (ROWS, ROWS), 0)
    source = lax.broadcasted_iota(jnp.int32, (ROWS, ROWS), 1)
    same = (row >= EDGE) == (source >= EDGE)
    shifter = (same & (source == row - delta[0])).astype(jnp.float32).astype(jnp.bfloat16)
    first_tile = partner * SPREAD + column
    wide = jnp.concatenate([boxes[first_tile + tile] for tile in range(TILES + 1)], axis=1)
    wide = jnp.dot(shifter, wide, preferred_element_type=jnp.float32)
    turned = [
        pltpu.roll(wide[:, tile * LANE : (tile + 1) * LANE], LANE - turn, 1)
        for tile in range(TILES + 1)
    ]
    for tile in range(TILES):
        span = slice(tile * LANE, (tile + 1) * LANE)
        second = cells[0:1, span] - delta[1]
        third = cells[1:2, span] - delta[2]
        inside = (second >= 0) & (second < EDGE) & (third >= 0) & (third < EDGE)
        inside = inside & (cells[0:1, span] >= 0)
        value = jnp.where(inside, jnp.where(keep, turned[tile], turned[tile + 1]), 0.0)
        product = boxes[center * SPREAD + EMPTY + tile].astype(jnp.float32) * value
        moved[pl.ds(pair_row, ROWS), span] = value
        density[pl.ds(pair_row, ROWS), span] = product.astype(jnp.bfloat16)


def by_chunk(body):
    for start in range(0, WIDTH, 256):
        body(start, min(256, WIDTH - start))


def solve(density, work, first, both, inverse, low, rows):
    span = slice(low, low + rows)
    for block in range(rows // (2 * ROWS)):
        part = slice(low + block * 2 * ROWS, low + (block + 1) * 2 * ROWS)
        work[part, :] = jnp.dot(
            first[...], density[part, :], preferred_element_type=jnp.float32
        ).astype(jnp.bfloat16)

    def forward(start, size):
        cut = pl.ds(start, size)
        out = jnp.dot(work[span, :], both[:, cut], preferred_element_type=jnp.float32)
        out = out.reshape(rows // ROWS, ROWS, size) * inverse[:, cut][None]
        density[span, cut] = out.reshape(rows, size).astype(jnp.bfloat16)

    def backward(start, size):
        cut = pl.ds(start, size)
        out = jnp.dot(density[span, :], both[:, cut], preferred_element_type=jnp.float32)
        work[span, cut] = out.astype(jnp.bfloat16)

    by_chunk(forward)
    by_chunk(backward)


def flatten_rows(lines, place):
    half = EDGE // 2
    lanes = lax.broadcasted_iota(jnp.int32, (half, LANE), 1)
    for spin in range(SPINS):
        even = [
            pltpu.roll(lines[tile, pl.ds(spin * EDGE, half, stride=2), :], LANE - OFF, 1)
            for tile in range(TILES)
        ]
        odd = [
            pltpu.roll(lines[tile, pl.ds(spin * EDGE + 1, half, stride=2), :], OFF, 1)
            for tile in range(TILES)
        ]
        for tile in range(TILES - 1):
            place(2 * tile + spin, jnp.where(lanes < LANE - OFF, even[tile], even[tile + 1]))
        place(2 * (TILES - 1) + spin, jnp.where(lanes < LANE // 2, even[TILES - 1], odd[0]))
        for tile in range(1, TILES):
            place(
                2 * (TILES - 1 + tile) + spin,
                jnp.where(lanes < OFF, odd[tile - 1], odd[tile]),
            )


def tile_spins(flat, ready):
    def group(number, carry):
        row = number * 2 * GROUP
        column = number * GROUP * LANE
        for tile in range(GROUP):
            start = pl.multiple_of(column + tile * LANE, LANE)
            ready[:, pl.ds(start, LANE)] = flat[pl.ds(row + 2 * tile, SPINS), :]
        return carry

    lax.fori_loop(0, CELLS // (GROUP * LANE), group, 0)


def mesh_place(device):
    gz = lax.axis_size(AXES[2])
    gy = lax.axis_size(AXES[1])
    return (device // (gy * gz), (device // gz) % gy, device % gz)


def solve_kernel(
    dest, partners, anchors, orbitals, first, both_hbm, inverse, cells,
    ready,
    boxes, moved, density, work, both, lines, flat, box_out, box_in, sends, arrived,
    table_sem, box_send, box_recv, move_send, move_recv,
):
    device = device_number()
    has_next = device < DEVICES - 1
    has_prev = device > 0
    following = mesh_place(jnp.minimum(device + 1, DEVICES - 1))
    previous = mesh_place(jnp.maximum(device - 1, 0))
    barrier = pltpu.get_barrier_semaphore()

    @pl.when(has_next)
    def _():
        pl.semaphore_signal(barrier, inc=1, device_id=following, device_id_type=MESH)

    @pl.when(has_prev)
    def _():
        pl.semaphore_signal(barrier, inc=1, device_id=previous, device_id_type=MESH)

    table = pltpu.make_async_copy(both_hbm, both, table_sem)
    table.start()

    def box_copy(way):
        return pltpu.make_async_remote_copy(
            src_ref=box_out.at[way], dst_ref=box_in.at[way],
            send_sem=box_send.at[way], recv_sem=box_recv.at[way],
            device_id=(following, previous)[way], device_id_type=MESH,
        )

    def move_copy(spot):
        return pltpu.make_async_remote_copy(
            src_ref=sends.at[spot], dst_ref=arrived.at[spot],
            send_sem=move_send.at[spot], recv_sem=move_recv.at[spot],
            device_id=previous if spot < 2 else following, device_id_type=MESH,
        )

    blank = jnp.zeros((ROWS, LANE), jnp.bfloat16)
    for box in range(BOX_DEV + 2):
        for tile in range(EMPTY):
            boxes[box * SPREAD + tile] = blank
            boxes[box * SPREAD + EMPTY + TILES + tile] = blank
    unpack_rows(orbitals, lines, boxes)
    for way, other in enumerate((device + 1, device - 1)):
        chosen = shared_box(partners, device, other)
        for tile in range(TILES):
            box_out[way, tile] = boxes[chosen * SPREAD + EMPTY + tile]

    pl.semaphore_wait(barrier, has_next.astype(jnp.int32) + has_prev.astype(jnp.int32))

    @pl.when(has_next)
    def _():
        box_copy(0).start()

    @pl.when(has_prev)
    def _():
        box_copy(1).start()

    order = boxes_by_position(dest, device)
    base = device * BOX_DEV

    @pl.when(has_prev)
    def _():
        box_copy(0).wait_recv()
        for tile in range(TILES):
            boxes[BOX_DEV * SPREAD + EMPTY + tile] = box_in[0, tile]

    @pl.when(has_next)
    def _():
        box_copy(1).wait_recv()
        for tile in range(TILES):
            boxes[(BOX_DEV + 1) * SPREAD + EMPTY + tile] = box_in[1, tile]

    def pair(number, carry):
        spot = number // 2
        which = number % 2
        local_box = pick(order, spot)
        box = base + local_box
        partner = partners[which, box]
        local = partner - base
        place = jnp.where(local < 0, 4, jnp.where(local >= BOX_DEV, 5, local))
        delta = [wrapped(anchors[dim, partner] - anchors[dim, box], GRID[dim]) for dim in range(3)]
        shift_pair(boxes, moved, density, cells, local_box, place, delta, number * ROWS)
        return carry

    lax.fori_loop(0, 2 * BOX_DEV, pair, 0)
    table.wait()
    for spot in range(BOX_DEV):
        solve(density, work, first, both, inverse, spot * 2 * ROWS, 2 * ROWS)
        span = slice(spot * 2 * ROWS, (spot + 1) * 2 * ROWS)
        potential = jnp.dot(first[...], work[span, :], preferred_element_type=jnp.float32)
        terms = potential * moved[span, :]
        total = terms[:ROWS] + terms[ROWS:]
        for tile in range(TILES):
            lines[tile, :ROWS, :] = total[:, tile * LANE : (tile + 1) * LANE]

        def place(row, value):
            flat[spot, pl.ds(row, EDGE // 2, stride=2 * (2 * TILES - 1)), :] = value

        flatten_rows(lines, place)
        if spot < 3:
            sends[spot] = flat[spot].astype(jnp.bfloat16)

            @pl.when(has_prev if spot < 2 else has_next)
            def _():
                move_copy(spot).start()

    for spot in range(BOX_DEV):
        tile_spins(flat.at[spot], ready.at[spot])
    for spot in (0, 2, 1):
        comes = has_next if spot < 2 else has_prev

        @pl.when(comes)
        def _():
            move_copy(spot).wait_recv()
            flat[spot] = arrived[spot].astype(jnp.float32)
            tile_spins(flat.at[spot], ready.at[BOX_DEV + spot])

    @pl.when(has_next)
    def _():
        box_copy(0).wait_send()
        move_copy(2).wait_send()

    @pl.when(has_prev)
    def _():
        box_copy(1).wait_send()
        move_copy(0).wait_send()
        move_copy(1).wait_send()


def assemble_kernel(dest, ready, out, blank, sems):
    device = device_number()
    blank[...] = jnp.zeros(blank.shape, jnp.float32)
    for slot, source in enumerate(slot_sources(dest, device)):

        @pl.when(source < CAP)
        def _():
            where = jnp.minimum(source, CAP - 1)
            pltpu.make_async_copy(ready.at[where], out.at[slot], sems.at[slot]).start()

        @pl.when(source == CAP)
        def _():
            pltpu.make_async_copy(blank, out.at[slot], sems.at[slot]).start()

    for slot in range(CAP):
        pltpu.make_async_copy(blank, out.at[slot], sems.at[slot]).wait()


VMEM_LIMIT = 36 * 1024 * 1024


def shards(orbitals, dest, partners, anchors):
    first, both, inverse, cells = (jnp.asarray(table) for table in tables())
    both = pltpu.with_memory_space_constraint(both, pltpu.HBM)
    partners = partners.T
    anchors = anchors.T
    smem = pl.BlockSpec(memory_space=pltpu.SMEM)
    vmem = pl.BlockSpec(memory_space=pltpu.VMEM)
    hbm = pl.BlockSpec(memory_space=pl.ANY)
    ready = pl.pallas_call(
        solve_kernel,
        out_shape=jax.ShapeDtypeStruct((CAP, SPINS, CELLS), jnp.float32),
        in_specs=[smem] * 3 + [vmem, vmem, pl.BlockSpec(memory_space=pltpu.HBM), vmem, vmem],
        out_specs=vmem,
        scratch_shapes=[
            pltpu.VMEM(((BOX_DEV + 2) * SPREAD, ROWS, LANE), jnp.bfloat16),
            pltpu.VMEM((PAIR_ROWS, WIDTH), jnp.float32),
            pltpu.VMEM((PAIR_ROWS, WIDTH), jnp.bfloat16),
            pltpu.VMEM((PAIR_ROWS, WIDTH), jnp.bfloat16),
            pltpu.VMEM((WIDTH, WIDTH), jnp.bfloat16),
            pltpu.VMEM((TILES, BOX_DEV * ROWS, LANE), jnp.float32),
            pltpu.VMEM((BOX_DEV, OUT_ROWS, LANE), jnp.float32),
            pltpu.VMEM((2, TILES, ROWS, LANE), jnp.bfloat16),
            pltpu.VMEM((2, TILES, ROWS, LANE), jnp.bfloat16),
            pltpu.VMEM((3, OUT_ROWS, LANE), jnp.bfloat16),
            pltpu.VMEM((3, OUT_ROWS, LANE), jnp.bfloat16),
            pltpu.SemaphoreType.DMA,
            pltpu.SemaphoreType.DMA((2,)),
            pltpu.SemaphoreType.DMA((2,)),
            pltpu.SemaphoreType.DMA((3,)),
            pltpu.SemaphoreType.DMA((3,)),
        ],
        compiler_params=pltpu.CompilerParams(
            vmem_limit_bytes=VMEM_LIMIT, collective_id=0, has_side_effects=True
        ),
    )(dest, partners, anchors, orbitals, first, both, inverse, cells)
    out = pl.pallas_call(
        assemble_kernel,
        out_shape=jax.ShapeDtypeStruct((CAP, SPINS, CELLS), jnp.float32),
        in_specs=[smem, hbm],
        out_specs=hbm,
        scratch_shapes=[
            pltpu.VMEM((SPINS, CELLS), jnp.float32),
            pltpu.SemaphoreType.DMA((CAP,)),
        ],
        compiler_params=pltpu.CompilerParams(vmem_limit_bytes=2 * 1024 * 1024),
    )(dest, ready)
    return jnp.transpose(out, (1, 0, 2))


def solution(mesh):
    return jax.shard_map(
        shards,
        mesh=mesh,
        in_specs=(P(None, AXES, None), P(), P(), P()),
        out_specs=P(None, AXES, None),
        check_vma=False,
    )
```

```python
import functools

import jax
import jax.numpy as jnp
import ml_dtypes
import numpy as np
from jax import lax
from jax.experimental import pallas as pl
from jax.experimental.pallas import tpu as pltpu
from jax.sharding import PartitionSpec as P

AXES = ("gx", "gy", "gz")
DEVICES = 128
BOXES = 512
SPINS = 2
EDGE = 40
PLANE = EDGE * EDGE
CELLS = EDGE * PLANE
GRID = (768, 384, 384)
BOX_DEV = 4
CAP = 7
SCREEN = 0.001

LANE = 128
TILES = 13
WIDTH = TILES * LANE
OFF = (WIDTH - PLANE) // 2
MARGIN = 7 * LANE
WIDE = WIDTH + 2 * MARGIN
ROWS = SPINS * EDGE
PAIR_ROWS = BOX_DEV * 2 * ROWS
OUT_ROWS = SPINS * CELLS // LANE
GROUP = 25
EMPTY = MARGIN // LANE
SPREAD = WIDE // LANE
MESH = pl.DeviceIdType.MESH


def tables():
    counter = np.arange(EDGE, dtype=np.float64) + 1.0
    angles = np.pi * counter[:, None] * counter[None, :] / (EDGE + 1.0)
    sine = (np.sqrt(2.0 / (EDGE + 1.0)) * np.sin(angles)).astype(ml_dtypes.bfloat16)
    levels = 2.0 - 2.0 * np.cos(np.pi * counter / (EDGE + 1.0))
    plane = (levels[:, None] + levels[None, :]).reshape(-1)
    inverse = np.zeros((EDGE, WIDTH), np.float32)
    inverse[:, OFF : OFF + PLANE] = 1.0 / (levels[:, None] + plane[None, :] + SCREEN)
    inverse = np.concatenate([inverse, inverse], axis=0)
    sine32 = sine.astype(np.float32)
    first = np.kron(np.eye(4, dtype=np.float32), sine32).astype(ml_dtypes.bfloat16)
    both = np.zeros((WIDTH, WIDTH), np.float32)
    both[OFF : OFF + PLANE, OFF : OFF + PLANE] = np.kron(sine32, sine32)
    both = both.astype(ml_dtypes.bfloat16)
    cells = np.full((2, WIDTH), -1000, np.int32)
    cells[0, OFF : OFF + PLANE] = np.arange(PLANE) // EDGE
    cells[1, OFF : OFF + PLANE] = np.arange(PLANE) % EDGE
    return first, both, inverse, cells


def device_number():
    index = lax.axis_index(AXES[0])
    for name in AXES[1:]:
        index = index * lax.axis_size(name) + lax.axis_index(name)
    return index


def count(dest, first_box, device):
    total = 0
    for number in range(BOX_DEV):
        total = total + (dest[first_box + number] == device).astype(jnp.int32)
    return total


def position(backs, aheads, rank):
    place = backs + rank
    return place + jnp.where((place >= 2) & (aheads > 0), 1, 0)


def boxes_by_position(dest, device):
    base = device * BOX_DEV
    backs = count(dest, base, device - 1)
    aheads = count(dest, base, device + 1)
    order = [0] * BOX_DEV
    back_rank = stay_rank = 0
    for number in range(BOX_DEV):
        goal = dest[base + number]
        back = goal < device
        ahead = goal > device
        place = jnp.where(back, back_rank, jnp.where(ahead, 2, position(backs, aheads, stay_rank)))
        back_rank = back_rank + back.astype(jnp.int32)
        stay_rank = stay_rank + (goal == device).astype(jnp.int32)
        for spot in range(BOX_DEV):
            order[spot] = order[spot] + jnp.where(place == spot, number, 0)
    return order


def slot_sources(dest, device):
    base = device * BOX_DEV
    last = DEVICES - 1
    backs = count(dest, base, device - 1)
    aheads = count(dest, base, device + 1)
    stays = BOX_DEV - backs - aheads
    behind = jnp.maximum(device - 1, 0) * BOX_DEV
    front = jnp.minimum(device + 1, last) * BOX_DEV
    from_prev = jnp.where(device > 0, count(dest, behind, device), 0)
    from_next = jnp.where(device < last, count(dest, front, device), 0)
    sources = []
    for slot in range(CAP):
        rank = slot - from_prev
        late = rank - stays
        sources.append(
            jnp.where(
                rank < 0,
                6,
                jnp.where(
                    late < 0,
                    position(backs, aheads, rank),
                    jnp.where(late < from_next, 4 + late, 7),
                ),
            )
        )
    return sources


def shared_box(partners, device, other):
    inside = jnp.clip(other, 0, DEVICES - 1) * BOX_DEV
    chosen = 0
    for number in range(BOX_DEV):
        for which in range(2):
            partner = partners[which, inside + number] - device * BOX_DEV
            chosen = jnp.where((partner >= 0) & (partner < BOX_DEV), partner, chosen)
    return chosen


def wrapped(difference, extent):
    half = difference + extent // 2
    half = jnp.where(half < 0, half + extent, half)
    half = jnp.where(half >= extent, half - extent, half)
    return half - extent // 2


def pick(values, index):
    chosen = values[0]
    for number in range(1, len(values)):
        chosen = jnp.where(index == number, values[number], chosen)
    return chosen


def unpack_rows(orbitals, lines, boxes):
    def pair(number, carry):
        start = pl.multiple_of(number * 2 * PLANE, LANE)
        for spin in range(SPINS):
            cells = orbitals[spin, :, pl.ds(start, 2 * PLANE)].astype(jnp.float32)
            even = pltpu.roll(cells[:, :WIDTH], OFF, 1)
            odd = pltpu.roll(cells[:, 2 * PLANE - WIDTH :], WIDTH - OFF, 1)
            row = spin * EDGE + 2 * number
            for tile in range(TILES):
                span = slice(tile * LANE, (tile + 1) * LANE)
                lines[tile, pl.ds(row, BOX_DEV, stride=ROWS), :] = even[:, span]
                lines[tile, pl.ds(row + 1, BOX_DEV, stride=ROWS), :] = odd[:, span]
        return carry

    lax.fori_loop(0, EDGE // 2, pair, 0, unroll=4)
    for box in range(BOX_DEV):
        for tile in range(TILES):
            value = lines[tile, box * ROWS : (box + 1) * ROWS, :]
            boxes[box * SPREAD + EMPTY + tile] = value.astype(jnp.bfloat16)


def shift_pair(boxes, moved, density, cells, center, partner, delta, pair_row):
    flat = MARGIN - (delta[1] * EDGE + delta[2])
    column = flat // LANE
    turn = flat - column * LANE
    keep = lax.broadcasted_iota(jnp.int32, (ROWS, LANE), 1) < LANE - turn
    row = lax.broadcasted_iota(jnp.int32, (ROWS, ROWS), 0)
    source = lax.broadcasted_iota(jnp.int32, (ROWS, ROWS), 1)
    same = (row >= EDGE) == (source >= EDGE)
    shifter = (same & (source == row - delta[0])).astype(jnp.float32).astype(jnp.bfloat16)
    first_tile = partner * SPREAD + column
    wide = jnp.concatenate([boxes[first_tile + tile] for tile in range(TILES + 1)], axis=1)
    wide = jnp.dot(shifter, wide, preferred_element_type=jnp.float32)
    turned = [
        pltpu.roll(wide[:, tile * LANE : (tile + 1) * LANE], LANE - turn, 1)
        for tile in range(TILES + 1)
    ]
    for tile in range(TILES):
        span = slice(tile * LANE, (tile + 1) * LANE)
        second = cells[0:1, span] - delta[1]
        third = cells[1:2, span] - delta[2]
        inside = (second >= 0) & (second < EDGE) & (third >= 0) & (third < EDGE)
        inside = inside & (cells[0:1, span] >= 0)
        value = jnp.where(inside, jnp.where(keep, turned[tile], turned[tile + 1]), 0.0)
        product = boxes[center * SPREAD + EMPTY + tile].astype(jnp.float32) * value
        moved[pair_row : pair_row + ROWS, span] = value
        density[pair_row : pair_row + ROWS, span] = product.astype(jnp.bfloat16)


def by_chunk(body):
    for start in range(0, WIDTH, 256):
        body(start, min(256, WIDTH - start))


def solve(density, work, first, both, inverse, low, rows):
    span = slice(low, low + rows)
    for block in range(rows // (2 * ROWS)):
        part = slice(low + block * 2 * ROWS, low + (block + 1) * 2 * ROWS)
        work[part, :] = jnp.dot(
            first[...], density[part, :], preferred_element_type=jnp.float32
        ).astype(jnp.bfloat16)

    def forward(start, size):
        cut = pl.ds(start, size)
        out = jnp.dot(work[span, :], both[:, cut], preferred_element_type=jnp.float32)
        out = out.reshape(rows // ROWS, ROWS, size) * inverse[:, cut][None]
        density[span, cut] = out.reshape(rows, size).astype(jnp.bfloat16)

    def backward(start, size):
        cut = pl.ds(start, size)
        out = jnp.dot(density[span, :], both[:, cut], preferred_element_type=jnp.float32)
        work[span, cut] = out.astype(jnp.bfloat16)

    by_chunk(forward)
    by_chunk(backward)


def flatten_rows(lines, place):
    half = EDGE // 2
    lanes = lax.broadcasted_iota(jnp.int32, (half, LANE), 1)
    for spin in range(SPINS):
        even = [
            pltpu.roll(lines[tile, pl.ds(spin * EDGE, half, stride=2), :], LANE - OFF, 1)
            for tile in range(TILES)
        ]
        odd = [
            pltpu.roll(lines[tile, pl.ds(spin * EDGE + 1, half, stride=2), :], OFF, 1)
            for tile in range(TILES)
        ]
        for tile in range(TILES - 1):
            place(2 * tile + spin, jnp.where(lanes < LANE - OFF, even[tile], even[tile + 1]))
        place(2 * (TILES - 1) + spin, jnp.where(lanes < LANE // 2, even[TILES - 1], odd[0]))
        for tile in range(1, TILES):
            place(
                2 * (TILES - 1 + tile) + spin,
                jnp.where(lanes < OFF, odd[tile - 1], odd[tile]),
            )


def tile_spins(flat, ready):
    def group(number, carry):
        row = number * 2 * GROUP
        column = number * GROUP * LANE
        for tile in range(GROUP):
            start = pl.multiple_of(column + tile * LANE, LANE)
            ready[:, pl.ds(start, LANE)] = flat[pl.ds(row + 2 * tile, SPINS), :]
        return carry

    lax.fori_loop(0, CELLS // (GROUP * LANE), group, 0)


def mesh_place(device):
    gz = lax.axis_size(AXES[2])
    gy = lax.axis_size(AXES[1])
    return (device // (gy * gz), (device // gz) % gy, device % gz)


def solve_kernel(
    dest_hbm, partners_hbm, anchors_hbm, orbitals_hbm, first_hbm, both_hbm, inverse_hbm, cells_hbm,
    ready,
    dest, partners, anchors, orbitals, first, inverse, cells,
    boxes, moved, density, work, both, lines, flat, box_out, box_in, sends, arrived,
    load_sems, box_send, box_recv, move_send, move_recv,
):
    device = device_number()
    has_next = device < DEVICES - 1
    has_prev = device > 0
    following = mesh_place(jnp.minimum(device + 1, DEVICES - 1))
    previous = mesh_place(jnp.maximum(device - 1, 0))
    barrier = pltpu.get_barrier_semaphore()

    @pl.when(has_next)
    def _():
        pl.semaphore_signal(barrier, inc=1, device_id=following, device_id_type=MESH)

    @pl.when(has_prev)
    def _():
        pl.semaphore_signal(barrier, inc=1, device_id=previous, device_id_type=MESH)

    loads = [
        pltpu.make_async_copy(source, target, load_sems.at[number])
        for number, (source, target) in enumerate(
            (
                (orbitals_hbm, orbitals),
                (dest_hbm, dest),
                (partners_hbm, partners),
                (anchors_hbm, anchors),
                (first_hbm, first),
                (cells_hbm, cells),
                (inverse_hbm, inverse),
                (both_hbm, both),
            )
        )
    ]
    for load in loads:
        load.start()

    def box_copy(way):
        return pltpu.make_async_remote_copy(
            src_ref=box_out.at[way], dst_ref=box_in.at[way],
            send_sem=box_send.at[way], recv_sem=box_recv.at[way],
            device_id=(following, previous)[way], device_id_type=MESH,
        )

    def move_copy(spot):
        return pltpu.make_async_remote_copy(
            src_ref=sends.at[spot], dst_ref=arrived.at[spot],
            send_sem=move_send.at[spot], recv_sem=move_recv.at[spot],
            device_id=previous if spot < 2 else following, device_id_type=MESH,
        )

    blank = jnp.zeros((ROWS, LANE), jnp.bfloat16)
    for box in range(BOX_DEV + 2):
        for tile in range(EMPTY):
            boxes[box * SPREAD + tile] = blank
            boxes[box * SPREAD + EMPTY + TILES + tile] = blank
    loads[0].wait()
    unpack_rows(orbitals, lines, boxes)
    for load in loads[1:4]:
        load.wait()
    for way, other in enumerate((device + 1, device - 1)):
        chosen = shared_box(partners, device, other)
        for tile in range(TILES):
            box_out[way, tile] = boxes[chosen * SPREAD + EMPTY + tile]

    pl.semaphore_wait(barrier, has_next.astype(jnp.int32) + has_prev.astype(jnp.int32))

    @pl.when(has_next)
    def _():
        box_copy(0).start()

    @pl.when(has_prev)
    def _():
        box_copy(1).start()

    order = boxes_by_position(dest, device)
    base = device * BOX_DEV

    @pl.when(has_prev)
    def _():
        box_copy(0).wait_recv()
        for tile in range(TILES):
            boxes[BOX_DEV * SPREAD + EMPTY + tile] = box_in[0, tile]

    @pl.when(has_next)
    def _():
        box_copy(1).wait_recv()
        for tile in range(TILES):
            boxes[(BOX_DEV + 1) * SPREAD + EMPTY + tile] = box_in[1, tile]

    def shift_box(spot):
        box = base + order[spot]
        for which in range(2):
            partner = partners[which, box]
            local = partner - base
            place = jnp.where(local < 0, 4, jnp.where(local >= BOX_DEV, 5, local))
            delta = [
                wrapped(anchors[dim, partner] - anchors[dim, box], GRID[dim]) for dim in range(3)
            ]
            row = (spot * 2 + which) * ROWS
            shift_pair(boxes, moved, density, cells, order[spot], place, delta, row)

    for load in loads[4:]:
        load.wait()
    shift_box(0)
    for spot in range(BOX_DEV):
        if spot + 1 < BOX_DEV:
            shift_box(spot + 1)
        solve(density, work, first, both, inverse, spot * 2 * ROWS, 2 * ROWS)
        span = slice(spot * 2 * ROWS, (spot + 1) * 2 * ROWS)
        potential = jnp.dot(first[...], work[span, :], preferred_element_type=jnp.float32)
        terms = potential * moved[span, :]
        total = terms[:ROWS] + terms[ROWS:]
        for tile in range(TILES):
            lines[tile, :ROWS, :] = total[:, tile * LANE : (tile + 1) * LANE]

        def place(row, value):
            flat[spot, pl.ds(row, EDGE // 2, stride=2 * (2 * TILES - 1)), :] = value

        flatten_rows(lines, place)
        if spot < 3:
            sends[spot] = flat[spot].astype(jnp.bfloat16)

            @pl.when(has_prev if spot < 2 else has_next)
            def _():
                move_copy(spot).start()

    for spot in range(BOX_DEV):
        tile_spins(flat.at[spot], ready.at[spot])
    for spot in (0, 2, 1):
        comes = has_next if spot < 2 else has_prev

        @pl.when(comes)
        def _():
            move_copy(spot).wait_recv()
            flat[spot] = arrived[spot].astype(jnp.float32)
            tile_spins(flat.at[spot], ready.at[BOX_DEV + spot])

    @pl.when(has_next)
    def _():
        box_copy(0).wait_send()
        move_copy(2).wait_send()

    @pl.when(has_prev)
    def _():
        box_copy(1).wait_send()
        move_copy(0).wait_send()
        move_copy(1).wait_send()


def assemble_kernel(dest, ready, out, blank, sems):
    device = device_number()
    blank[...] = jnp.zeros(blank.shape, jnp.float32)
    for slot, source in enumerate(slot_sources(dest, device)):

        @pl.when(source < CAP)
        def _():
            where = jnp.minimum(source, CAP - 1)
            pltpu.make_async_copy(ready.at[where], out.at[slot], sems.at[slot]).start()

        @pl.when(source == CAP)
        def _():
            pltpu.make_async_copy(blank, out.at[slot], sems.at[slot]).start()

    for slot in range(CAP):
        pltpu.make_async_copy(blank, out.at[slot], sems.at[slot]).wait()


VMEM_LIMIT = 36 * 1024 * 1024


def shards(orbitals, dest, partners, anchors):
    first, both, inverse, cells = (jnp.asarray(table) for table in tables())
    operands = (dest, partners.T, anchors.T, orbitals, first, both, inverse, cells)
    operands = [pltpu.with_memory_space_constraint(operand, pltpu.HBM) for operand in operands]
    smem = pl.BlockSpec(memory_space=pltpu.SMEM)
    vmem = pl.BlockSpec(memory_space=pltpu.VMEM)
    hbm = pl.BlockSpec(memory_space=pl.ANY)
    ready = pl.pallas_call(
        solve_kernel,
        out_shape=jax.ShapeDtypeStruct((CAP, SPINS, CELLS), jnp.float32),
        in_specs=[pl.BlockSpec(memory_space=pltpu.HBM)] * 8,
        out_specs=vmem,
        scratch_shapes=[
            pltpu.SMEM((BOXES,), jnp.int32),
            pltpu.SMEM((2, BOXES), jnp.int32),
            pltpu.SMEM((3, BOXES), jnp.int32),
            pltpu.VMEM((SPINS, BOX_DEV, CELLS), jnp.bfloat16),
            pltpu.VMEM(first.shape, first.dtype),
            pltpu.VMEM(inverse.shape, inverse.dtype),
            pltpu.VMEM(cells.shape, cells.dtype),
            pltpu.VMEM(((BOX_DEV + 2) * SPREAD, ROWS, LANE), jnp.bfloat16),
            pltpu.VMEM((PAIR_ROWS, WIDTH), jnp.float32),
            pltpu.VMEM((PAIR_ROWS, WIDTH), jnp.bfloat16),
            pltpu.VMEM((PAIR_ROWS, WIDTH), jnp.bfloat16),
            pltpu.VMEM((WIDTH, WIDTH), jnp.bfloat16),
            pltpu.VMEM((TILES, BOX_DEV * ROWS, LANE), jnp.float32),
            pltpu.VMEM((BOX_DEV, OUT_ROWS, LANE), jnp.float32),
            pltpu.VMEM((2, TILES, ROWS, LANE), jnp.bfloat16),
            pltpu.VMEM((2, TILES, ROWS, LANE), jnp.bfloat16),
            pltpu.VMEM((3, OUT_ROWS, LANE), jnp.bfloat16),
            pltpu.VMEM((3, OUT_ROWS, LANE), jnp.bfloat16),
            pltpu.SemaphoreType.DMA((8,)),
            pltpu.SemaphoreType.DMA((2,)),
            pltpu.SemaphoreType.DMA((2,)),
            pltpu.SemaphoreType.DMA((3,)),
            pltpu.SemaphoreType.DMA((3,)),
        ],
        compiler_params=pltpu.CompilerParams(
            vmem_limit_bytes=VMEM_LIMIT, collective_id=0, has_side_effects=True
        ),
    )(*operands)
    out = pl.pallas_call(
        assemble_kernel,
        out_shape=jax.ShapeDtypeStruct((CAP, SPINS, CELLS), jnp.float32),
        in_specs=[smem, hbm],
        out_specs=hbm,
        scratch_shapes=[
            pltpu.VMEM((SPINS, CELLS), jnp.float32),
            pltpu.SemaphoreType.DMA((CAP,)),
        ],
        compiler_params=pltpu.CompilerParams(vmem_limit_bytes=2 * 1024 * 1024),
    )(dest, ready)
    return jnp.transpose(out, (1, 0, 2))


def solution(mesh):
    return jax.shard_map(
        shards,
        mesh=mesh,
        in_specs=(P(None, AXES, None), P(), P(), P()),
        out_specs=P(None, AXES, None),
        check_vma=False,
    )
```

```python
import functools

import jax
import jax.numpy as jnp
import ml_dtypes
import numpy as np
from jax import lax
from jax.experimental import pallas as pl
from jax.experimental.pallas import tpu as pltpu
from jax.sharding import PartitionSpec as P

AXES = ("gx", "gy", "gz")
DEVICES = 128
BOXES = 512
SPINS = 2
EDGE = 40
PLANE = EDGE * EDGE
CELLS = EDGE * PLANE
GRID = (768, 384, 384)
BOX_DEV = 4
CAP = 7
SCREEN = 0.001

LANE = 128
TILES = 13
WIDTH = TILES * LANE
FOLDED = TILES // 2
HALF = (FOLDED + 1) * LANE
OFF = (WIDTH - PLANE) // 2
MARGIN = 7 * LANE
WIDE = WIDTH + 2 * MARGIN
ROWS = SPINS * EDGE
PAIR_ROWS = BOX_DEV * 2 * ROWS
OUT_ROWS = SPINS * CELLS // LANE
GROUP = 25
EMPTY = MARGIN // LANE
SPREAD = WIDE // LANE
MESH = pl.DeviceIdType.MESH


def tables():
    counter = np.arange(EDGE, dtype=np.float64) + 1.0
    angles = np.pi * counter[:, None] * counter[None, :] / (EDGE + 1.0)
    sine = (np.sqrt(2.0 / (EDGE + 1.0)) * np.sin(angles)).astype(ml_dtypes.bfloat16)
    levels = 2.0 - 2.0 * np.cos(np.pi * counter / (EDGE + 1.0))
    plane = (levels[:, None] + levels[None, :]).reshape(-1)
    inverse = np.zeros((EDGE, WIDTH), np.float32)
    inverse[:, OFF : OFF + PLANE] = 1.0 / (levels[:, None] + plane[None, :] + SCREEN)
    inverse = np.concatenate([inverse, inverse], axis=0)
    sine32 = sine.astype(np.float32)
    first = np.kron(np.eye(4, dtype=np.float32), sine32).astype(ml_dtypes.bfloat16)
    plane_sine = np.zeros((WIDTH, PLANE), np.float32)
    plane_sine[OFF : OFF + PLANE] = np.kron(sine32, sine32)
    mode = np.arange(PLANE)
    odd = (mode // EDGE + mode % EDGE) % 2
    both = np.zeros((2, 2, HALF, HALF), np.float32)
    scale = np.zeros((2 * EDGE, 2 * HALF), np.float32)
    for parity in range(2):
        chosen = mode[odd == parity]
        both[parity, 0, :, : chosen.size] = plane_sine[:HALF, chosen]
        both[parity, 1] = both[parity, 0].T
        scale[:, parity * HALF : parity * HALF + chosen.size] = inverse[:, OFF + chosen]
    inverse = scale
    both = both.reshape(4 * HALF, HALF).astype(ml_dtypes.bfloat16)
    cells = np.full((2, WIDTH), -1000, np.int32)
    cells[0, OFF : OFF + PLANE] = np.arange(PLANE) // EDGE
    cells[1, OFF : OFF + PLANE] = np.arange(PLANE) % EDGE
    return first, both, inverse, cells


def device_number():
    index = lax.axis_index(AXES[0])
    for name in AXES[1:]:
        index = index * lax.axis_size(name) + lax.axis_index(name)
    return index


def count(dest, first_box, device):
    total = 0
    for number in range(BOX_DEV):
        total = total + (dest[first_box + number] == device).astype(jnp.int32)
    return total


def position(backs, aheads, rank):
    place = backs + rank
    return place + jnp.where((place >= 2) & (aheads > 0), 1, 0)


def boxes_by_position(dest, device):
    base = device * BOX_DEV
    backs = count(dest, base, device - 1)
    aheads = count(dest, base, device + 1)
    order = [0] * BOX_DEV
    back_rank = stay_rank = 0
    for number in range(BOX_DEV):
        goal = dest[base + number]
        back = goal < device
        ahead = goal > device
        place = jnp.where(back, back_rank, jnp.where(ahead, 2, position(backs, aheads, stay_rank)))
        back_rank = back_rank + back.astype(jnp.int32)
        stay_rank = stay_rank + (goal == device).astype(jnp.int32)
        for spot in range(BOX_DEV):
            order[spot] = order[spot] + jnp.where(place == spot, number, 0)
    return order


def slot_sources(dest, device):
    base = device * BOX_DEV
    last = DEVICES - 1
    backs = count(dest, base, device - 1)
    aheads = count(dest, base, device + 1)
    stays = BOX_DEV - backs - aheads
    behind = jnp.maximum(device - 1, 0) * BOX_DEV
    front = jnp.minimum(device + 1, last) * BOX_DEV
    from_prev = jnp.where(device > 0, count(dest, behind, device), 0)
    from_next = jnp.where(device < last, count(dest, front, device), 0)
    sources = []
    for slot in range(CAP):
        rank = slot - from_prev
        late = rank - stays
        sources.append(
            jnp.where(
                rank < 0,
                6,
                jnp.where(
                    late < 0,
                    position(backs, aheads, rank),
                    jnp.where(late < from_next, 4 + late, 7),
                ),
            )
        )
    return sources


def shared_box(partners, device, other):
    inside = jnp.clip(other, 0, DEVICES - 1) * BOX_DEV
    chosen = 0
    for number in range(BOX_DEV):
        for which in range(2):
            partner = partners[which, inside + number] - device * BOX_DEV
            chosen = jnp.where((partner >= 0) & (partner < BOX_DEV), partner, chosen)
    return chosen


def wrapped(difference, extent):
    half = difference + extent // 2
    half = jnp.where(half < 0, half + extent, half)
    half = jnp.where(half >= extent, half - extent, half)
    return half - extent // 2


def pick(values, index):
    chosen = values[0]
    for number in range(1, len(values)):
        chosen = jnp.where(index == number, values[number], chosen)
    return chosen


def unpack_rows(orbitals, lines, boxes):
    def pair(number, carry):
        start = pl.multiple_of(number * 2 * PLANE, LANE)
        for spin in range(SPINS):
            cells = orbitals[spin, :, pl.ds(start, 2 * PLANE)].astype(jnp.float32)
            even = pltpu.roll(cells[:, :WIDTH], OFF, 1)
            odd = pltpu.roll(cells[:, 2 * PLANE - WIDTH :], WIDTH - OFF, 1)
            row = spin * EDGE + 2 * number
            for tile in range(TILES):
                span = slice(tile * LANE, (tile + 1) * LANE)
                lines[tile, pl.ds(row, BOX_DEV, stride=ROWS), :] = even[:, span]
                lines[tile, pl.ds(row + 1, BOX_DEV, stride=ROWS), :] = odd[:, span]
        return carry

    lax.fori_loop(0, EDGE // 2, pair, 0, unroll=4)
    for box in range(BOX_DEV):
        for tile in range(TILES):
            value = lines[tile, box * ROWS : (box + 1) * ROWS, :]
            boxes[box * SPREAD + EMPTY + tile] = value.astype(jnp.bfloat16)


def shift_pair(boxes, moved, density, cells, center, partner, delta, pair_row):
    flat = MARGIN - (delta[1] * EDGE + delta[2])
    column = flat // LANE
    turn = flat - column * LANE
    keep = lax.broadcasted_iota(jnp.int32, (ROWS, LANE), 1) < LANE - turn
    row = lax.broadcasted_iota(jnp.int32, (ROWS, ROWS), 0)
    source = lax.broadcasted_iota(jnp.int32, (ROWS, ROWS), 1)
    same = (row >= EDGE) == (source >= EDGE)
    shifter = (same & (source == row - delta[0])).astype(jnp.float32).astype(jnp.bfloat16)
    first_tile = partner * SPREAD + column
    wide = jnp.concatenate([boxes[first_tile + tile] for tile in range(TILES + 1)], axis=1)
    wide = jnp.dot(shifter, wide, preferred_element_type=jnp.float32)
    turned = [
        pltpu.roll(wide[:, tile * LANE : (tile + 1) * LANE], LANE - turn, 1)
        for tile in range(TILES + 1)
    ]
    for tile in range(TILES):
        span = slice(tile * LANE, (tile + 1) * LANE)
        second = cells[0:1, span] - delta[1]
        third = cells[1:2, span] - delta[2]
        inside = (second >= 0) & (second < EDGE) & (third >= 0) & (third < EDGE)
        inside = inside & (cells[0:1, span] >= 0)
        value = jnp.where(inside, jnp.where(keep, turned[tile], turned[tile + 1]), 0.0)
        product = boxes[center * SPREAD + EMPTY + tile].astype(jnp.float32) * value
        moved[pair_row : pair_row + ROWS, span] = value
        density[pair_row : pair_row + ROWS, span] = product.astype(jnp.bfloat16)


def mirrored(value):
    lanes = LANE - 1 - lax.broadcasted_iota(jnp.int32, value.shape, 1)
    return jnp.take_along_axis(value, lanes, axis=1)


def tile_of(value, tile):
    return value[:, tile * LANE : (tile + 1) * LANE]


def solve(density, work, folded, modes, first, both, inverse, low):
    rows = slice(low, low + 2 * ROWS)
    value = jnp.dot(first[...], density[rows, :], preferred_element_type=jnp.float32)
    for tile in range(FOLDED):
        here = tile_of(value, tile)
        there = mirrored(tile_of(value, TILES - 1 - tile))
        span = slice(tile * LANE, (tile + 1) * LANE)
        folded[0, rows, span] = (here + there).astype(jnp.bfloat16)
        folded[1, rows, span] = (here - there).astype(jnp.bfloat16)
    middle = tile_of(value, FOLDED).astype(jnp.bfloat16)
    for parity in range(2):
        folded[parity, rows, FOLDED * LANE :] = middle
    for parity in range(2):
        for start in range(0, HALF, 256):
            stop = min(start + 256, HALF)
            table = both[2 * parity * HALF : (2 * parity + 1) * HALF, start:stop]
            out = jnp.dot(folded[parity, rows, :], table, preferred_element_type=jnp.float32)
            scale = inverse[:, parity * HALF + start : parity * HALF + stop]
            out = out * jnp.concatenate([scale, scale], axis=0)
            modes[parity, rows, start:stop] = out.astype(jnp.bfloat16)
    for start in range(0, HALF, 256):
        stop = min(start + 256, HALF)
        even, odd = (
            jnp.dot(
                modes[parity, rows, :],
                both[(2 * parity + 1) * HALF : (2 * parity + 2) * HALF, start:stop],
                preferred_element_type=jnp.float32,
            )
            for parity in range(2)
        )
        work[rows, start:stop] = (even + odd).astype(jnp.bfloat16)
        for tile in range(start // LANE, min(stop // LANE, FOLDED)):
            inside = slice(tile * LANE - start, (tile + 1) * LANE - start)
            mirror = mirrored(even[:, inside] - odd[:, inside]).astype(jnp.bfloat16)
            target = TILES - 1 - tile
            work[rows, target * LANE : (target + 1) * LANE] = mirror


def flatten_rows(lines, place):
    half = EDGE // 2
    lanes = lax.broadcasted_iota(jnp.int32, (half, LANE), 1)
    for spin in range(SPINS):
        even = [
            pltpu.roll(lines[tile, pl.ds(spin * EDGE, half, stride=2), :], LANE - OFF, 1)
            for tile in range(TILES)
        ]
        odd = [
            pltpu.roll(lines[tile, pl.ds(spin * EDGE + 1, half, stride=2), :], OFF, 1)
            for tile in range(TILES)
        ]
        for tile in range(TILES - 1):
            place(2 * tile + spin, jnp.where(lanes < LANE - OFF, even[tile], even[tile + 1]))
        place(2 * (TILES - 1) + spin, jnp.where(lanes < LANE // 2, even[TILES - 1], odd[0]))
        for tile in range(1, TILES):
            place(
                2 * (TILES - 1 + tile) + spin,
                jnp.where(lanes < OFF, odd[tile - 1], odd[tile]),
            )


def tile_spins(flat, ready):
    def group(number, carry):
        row = number * 2 * GROUP
        column = number * GROUP * LANE
        for tile in range(GROUP):
            start = pl.multiple_of(column + tile * LANE, LANE)
            ready[:, pl.ds(start, LANE)] = flat[pl.ds(row + 2 * tile, SPINS), :]
        return carry

    lax.fori_loop(0, CELLS // (GROUP * LANE), group, 0)


def mesh_place(device):
    gz = lax.axis_size(AXES[2])
    gy = lax.axis_size(AXES[1])
    return (device // (gy * gz), (device // gz) % gy, device % gz)


def solve_kernel(
    dest_hbm, partners_hbm, anchors_hbm, orbitals_hbm, first_hbm, both_hbm, inverse_hbm, cells_hbm,
    ready,
    dest, partners, anchors, orbitals, first, inverse, cells,
    boxes, moved, density, work, folded, modes, both, lines, flat, box_out, box_in, sends, arrived,
    load_sems, box_send, box_recv, move_send, move_recv,
):
    device = device_number()
    has_next = device < DEVICES - 1
    has_prev = device > 0
    following = mesh_place(jnp.minimum(device + 1, DEVICES - 1))
    previous = mesh_place(jnp.maximum(device - 1, 0))
    barrier = pltpu.get_barrier_semaphore()

    @pl.when(has_next)
    def _():
        pl.semaphore_signal(barrier, inc=1, device_id=following, device_id_type=MESH)

    @pl.when(has_prev)
    def _():
        pl.semaphore_signal(barrier, inc=1, device_id=previous, device_id_type=MESH)

    loads = [
        pltpu.make_async_copy(source, target, load_sems.at[number])
        for number, (source, target) in enumerate(
            (
                (orbitals_hbm, orbitals),
                (dest_hbm, dest),
                (partners_hbm, partners),
                (anchors_hbm, anchors),
                (first_hbm, first),
                (cells_hbm, cells),
                (inverse_hbm, inverse),
                (both_hbm, both),
            )
        )
    ]
    for load in loads:
        load.start()

    def box_copy(way):
        return pltpu.make_async_remote_copy(
            src_ref=box_out.at[way], dst_ref=box_in.at[way],
            send_sem=box_send.at[way], recv_sem=box_recv.at[way],
            device_id=(following, previous)[way], device_id_type=MESH,
        )

    def move_copy(spot):
        return pltpu.make_async_remote_copy(
            src_ref=sends.at[spot], dst_ref=arrived.at[spot],
            send_sem=move_send.at[spot], recv_sem=move_recv.at[spot],
            device_id=previous if spot < 2 else following, device_id_type=MESH,
        )

    blank = jnp.zeros((ROWS, LANE), jnp.bfloat16)
    for box in range(BOX_DEV + 2):
        for tile in range(EMPTY):
            boxes[box * SPREAD + tile] = blank
            boxes[box * SPREAD + EMPTY + TILES + tile] = blank
    loads[0].wait()
    unpack_rows(orbitals, lines, boxes)
    for load in loads[1:4]:
        load.wait()
    for way, other in enumerate((device + 1, device - 1)):
        chosen = shared_box(partners, device, other)
        for tile in range(TILES):
            box_out[way, tile] = boxes[chosen * SPREAD + EMPTY + tile]

    pl.semaphore_wait(barrier, has_next.astype(jnp.int32) + has_prev.astype(jnp.int32))

    @pl.when(has_next)
    def _():
        box_copy(0).start()

    @pl.when(has_prev)
    def _():
        box_copy(1).start()

    order = boxes_by_position(dest, device)
    base = device * BOX_DEV

    @pl.when(has_prev)
    def _():
        box_copy(0).wait_recv()
        for tile in range(TILES):
            boxes[BOX_DEV * SPREAD + EMPTY + tile] = box_in[0, tile]

    @pl.when(has_next)
    def _():
        box_copy(1).wait_recv()
        for tile in range(TILES):
            boxes[(BOX_DEV + 1) * SPREAD + EMPTY + tile] = box_in[1, tile]

    def shift_box(spot):
        box = base + order[spot]
        for which in range(2):
            partner = partners[which, box]
            local = partner - base
            place = jnp.where(local < 0, 4, jnp.where(local >= BOX_DEV, 5, local))
            delta = [
                wrapped(anchors[dim, partner] - anchors[dim, box], GRID[dim]) for dim in range(3)
            ]
            row = (spot * 2 + which) * ROWS
            shift_pair(boxes, moved, density, cells, order[spot], place, delta, row)

    for load in loads[4:]:
        load.wait()
    shift_box(0)
    for spot in range(BOX_DEV):
        if spot + 1 < BOX_DEV:
            shift_box(spot + 1)
        solve(density, work, folded, modes, first, both, inverse, spot * 2 * ROWS)
        span = slice(spot * 2 * ROWS, (spot + 1) * 2 * ROWS)
        potential = jnp.dot(first[...], work[span, :], preferred_element_type=jnp.float32)
        terms = potential * moved[span, :]
        total = terms[:ROWS] + terms[ROWS:]
        for tile in range(TILES):
            lines[tile, :ROWS, :] = total[:, tile * LANE : (tile + 1) * LANE]

        def place(row, value):
            flat[spot, pl.ds(row, EDGE // 2, stride=2 * (2 * TILES - 1)), :] = value

        flatten_rows(lines, place)
        if spot < 3:
            sends[spot] = flat[spot].astype(jnp.bfloat16)

            @pl.when(has_prev if spot < 2 else has_next)
            def _():
                move_copy(spot).start()

    for spot in range(BOX_DEV):
        tile_spins(flat.at[spot], ready.at[spot])
    for spot in (0, 2, 1):
        comes = has_next if spot < 2 else has_prev

        @pl.when(comes)
        def _():
            move_copy(spot).wait_recv()
            flat[spot] = arrived[spot].astype(jnp.float32)
            tile_spins(flat.at[spot], ready.at[BOX_DEV + spot])

    @pl.when(has_next)
    def _():
        box_copy(0).wait_send()
        move_copy(2).wait_send()

    @pl.when(has_prev)
    def _():
        box_copy(1).wait_send()
        move_copy(0).wait_send()
        move_copy(1).wait_send()


def assemble_kernel(dest, ready, out, blank, sems):
    device = device_number()
    blank[...] = jnp.zeros(blank.shape, jnp.float32)
    for slot, source in enumerate(slot_sources(dest, device)):

        @pl.when(source < CAP)
        def _():
            where = jnp.minimum(source, CAP - 1)
            pltpu.make_async_copy(ready.at[where], out.at[slot], sems.at[slot]).start()

        @pl.when(source == CAP)
        def _():
            pltpu.make_async_copy(blank, out.at[slot], sems.at[slot]).start()

    for slot in range(CAP):
        pltpu.make_async_copy(blank, out.at[slot], sems.at[slot]).wait()


VMEM_LIMIT = 42 * 1024 * 1024


def shards(orbitals, dest, partners, anchors):
    first, both, inverse, cells = (jnp.asarray(table) for table in tables())
    operands = (dest, partners.T, anchors.T, orbitals, first, both, inverse, cells)
    operands = [pltpu.with_memory_space_constraint(operand, pltpu.HBM) for operand in operands]
    smem = pl.BlockSpec(memory_space=pltpu.SMEM)
    vmem = pl.BlockSpec(memory_space=pltpu.VMEM)
    hbm = pl.BlockSpec(memory_space=pl.ANY)
    ready = pl.pallas_call(
        solve_kernel,
        out_shape=jax.ShapeDtypeStruct((CAP, SPINS, CELLS), jnp.float32),
        in_specs=[pl.BlockSpec(memory_space=pltpu.HBM)] * 8,
        out_specs=vmem,
        scratch_shapes=[
            pltpu.SMEM((BOXES,), jnp.int32),
            pltpu.SMEM((2, BOXES), jnp.int32),
            pltpu.SMEM((3, BOXES), jnp.int32),
            pltpu.VMEM((SPINS, BOX_DEV, CELLS), jnp.bfloat16),
            pltpu.VMEM(first.shape, first.dtype),
            pltpu.VMEM(inverse.shape, inverse.dtype),
            pltpu.VMEM(cells.shape, cells.dtype),
            pltpu.VMEM(((BOX_DEV + 2) * SPREAD, ROWS, LANE), jnp.bfloat16),
            pltpu.VMEM((PAIR_ROWS, WIDTH), jnp.float32),
            pltpu.VMEM((PAIR_ROWS, WIDTH), jnp.bfloat16),
            pltpu.VMEM((PAIR_ROWS, WIDTH), jnp.bfloat16),
            pltpu.VMEM((2, PAIR_ROWS, HALF), jnp.bfloat16),
            pltpu.VMEM((2, PAIR_ROWS, HALF), jnp.bfloat16),
            pltpu.VMEM(both.shape, both.dtype),
            pltpu.VMEM((TILES, BOX_DEV * ROWS, LANE), jnp.float32),
            pltpu.VMEM((BOX_DEV, OUT_ROWS, LANE), jnp.float32),
            pltpu.VMEM((2, TILES, ROWS, LANE), jnp.bfloat16),
            pltpu.VMEM((2, TILES, ROWS, LANE), jnp.bfloat16),
            pltpu.VMEM((3, OUT_ROWS, LANE), jnp.bfloat16),
            pltpu.VMEM((3, OUT_ROWS, LANE), jnp.bfloat16),
            pltpu.SemaphoreType.DMA((8,)),
            pltpu.SemaphoreType.DMA((2,)),
            pltpu.SemaphoreType.DMA((2,)),
            pltpu.SemaphoreType.DMA((3,)),
            pltpu.SemaphoreType.DMA((3,)),
        ],
        compiler_params=pltpu.CompilerParams(
            vmem_limit_bytes=VMEM_LIMIT, collective_id=0, has_side_effects=True
        ),
    )(*operands)
    out = pl.pallas_call(
        assemble_kernel,
        out_shape=jax.ShapeDtypeStruct((CAP, SPINS, CELLS), jnp.float32),
        in_specs=[smem, hbm],
        out_specs=hbm,
        scratch_shapes=[
            pltpu.VMEM((SPINS, CELLS), jnp.float32),
            pltpu.SemaphoreType.DMA((CAP,)),
        ],
        compiler_params=pltpu.CompilerParams(vmem_limit_bytes=2 * 1024 * 1024),
    )(dest, ready)
    return jnp.transpose(out, (1, 0, 2))


def solution(mesh):
    return jax.shard_map(
        shards,
        mesh=mesh,
        in_specs=(P(None, AXES, None), P(), P(), P()),
        out_specs=P(None, AXES, None),
        check_vma=False,
    )
```

```python
import functools

import jax
import jax.numpy as jnp
import ml_dtypes
import numpy as np
from jax import lax
from jax.experimental import pallas as pl
from jax.experimental.pallas import tpu as pltpu
from jax.sharding import PartitionSpec as P

AXES = ("gx", "gy", "gz")
DEVICES = 128
BOXES = 512
SPINS = 2
EDGE = 40
PLANE = EDGE * EDGE
CELLS = EDGE * PLANE
GRID = (768, 384, 384)
BOX_DEV = 4
CAP = 7
SCREEN = 0.001

LANE = 128
TILES = 13
WIDTH = TILES * LANE
FOLDED = TILES // 2
HALF = (FOLDED + 1) * LANE
OFF = (WIDTH - PLANE) // 2
MARGIN = 7 * LANE
WIDE = WIDTH + 2 * MARGIN
ROWS = SPINS * EDGE
PAIR_ROWS = BOX_DEV * 2 * ROWS
OUT_ROWS = SPINS * CELLS // LANE
GROUP = 25
TURNS = (0, 2, 1, 3)
EMPTY = MARGIN // LANE
SPREAD = WIDE // LANE
MESH = pl.DeviceIdType.MESH


def tables():
    counter = np.arange(EDGE, dtype=np.float64) + 1.0
    angles = np.pi * counter[:, None] * counter[None, :] / (EDGE + 1.0)
    sine = (np.sqrt(2.0 / (EDGE + 1.0)) * np.sin(angles)).astype(ml_dtypes.bfloat16)
    levels = 2.0 - 2.0 * np.cos(np.pi * counter / (EDGE + 1.0))
    plane = (levels[:, None] + levels[None, :]).reshape(-1)
    inverse = np.zeros((EDGE, WIDTH), np.float32)
    inverse[:, OFF : OFF + PLANE] = 1.0 / (levels[:, None] + plane[None, :] + SCREEN)
    inverse = np.concatenate([inverse, inverse], axis=0)
    sine32 = sine.astype(np.float32)
    first = np.kron(np.eye(4, dtype=np.float32), sine32).astype(ml_dtypes.bfloat16)
    plane_sine = np.zeros((WIDTH, PLANE), np.float32)
    plane_sine[OFF : OFF + PLANE] = np.kron(sine32, sine32)
    mode = np.arange(PLANE)
    odd = (mode // EDGE + mode % EDGE) % 2
    both = np.zeros((2, 2, HALF, HALF), np.float32)
    scale = np.zeros((2 * EDGE, 2 * HALF), np.float32)
    for parity in range(2):
        chosen = mode[odd == parity]
        both[parity, 0, :, : chosen.size] = plane_sine[:HALF, chosen]
        both[parity, 1] = both[parity, 0].T
        scale[:, parity * HALF : parity * HALF + chosen.size] = inverse[:, OFF + chosen]
    inverse = scale
    both = both.reshape(4 * HALF, HALF).astype(ml_dtypes.bfloat16)
    cells = np.full((2, WIDTH), -1000, np.int32)
    cells[0, OFF : OFF + PLANE] = np.arange(PLANE) // EDGE
    cells[1, OFF : OFF + PLANE] = np.arange(PLANE) % EDGE
    return first, both, inverse, cells


def device_number():
    index = lax.axis_index(AXES[0])
    for name in AXES[1:]:
        index = index * lax.axis_size(name) + lax.axis_index(name)
    return index


def count(dest, first_box, device):
    total = 0
    for number in range(BOX_DEV):
        total = total + (dest[first_box + number] == device).astype(jnp.int32)
    return total


def position(backs, aheads, rank):
    place = backs + rank
    return place + jnp.where((place >= 2) & (aheads > 0), 1, 0)


def boxes_by_position(dest, device):
    base = device * BOX_DEV
    backs = count(dest, base, device - 1)
    aheads = count(dest, base, device + 1)
    order = [0] * BOX_DEV
    back_rank = stay_rank = 0
    for number in range(BOX_DEV):
        goal = dest[base + number]
        back = goal < device
        ahead = goal > device
        place = jnp.where(back, back_rank, jnp.where(ahead, 2, position(backs, aheads, stay_rank)))
        back_rank = back_rank + back.astype(jnp.int32)
        stay_rank = stay_rank + (goal == device).astype(jnp.int32)
        for spot in range(BOX_DEV):
            order[spot] = order[spot] + jnp.where(place == spot, number, 0)
    return order


def slot_sources(dest, device):
    base = device * BOX_DEV
    last = DEVICES - 1
    backs = count(dest, base, device - 1)
    aheads = count(dest, base, device + 1)
    stays = BOX_DEV - backs - aheads
    behind = jnp.maximum(device - 1, 0) * BOX_DEV
    front = jnp.minimum(device + 1, last) * BOX_DEV
    from_prev = jnp.where(device > 0, count(dest, behind, device), 0)
    from_next = jnp.where(device < last, count(dest, front, device), 0)
    sources = []
    for slot in range(CAP):
        rank = slot - from_prev
        late = rank - stays
        sources.append(
            jnp.where(
                rank < 0,
                6,
                jnp.where(
                    late < 0,
                    position(backs, aheads, rank),
                    jnp.where(late < from_next, 4 + late, 7),
                ),
            )
        )
    return sources


def shared_box(partners, device, other):
    inside = jnp.clip(other, 0, DEVICES - 1) * BOX_DEV
    chosen = 0
    for number in range(BOX_DEV):
        for which in range(2):
            partner = partners[which, inside + number] - device * BOX_DEV
            chosen = jnp.where((partner >= 0) & (partner < BOX_DEV), partner, chosen)
    return chosen


def wrapped(difference, extent):
    half = difference + extent // 2
    half = jnp.where(half < 0, half + extent, half)
    half = jnp.where(half >= extent, half - extent, half)
    return half - extent // 2


def pick(values, index):
    chosen = values[0]
    for number in range(1, len(values)):
        chosen = jnp.where(index == number, values[number], chosen)
    return chosen


def unpack_rows(spin, orbitals, lines):
    def pair(number, carry):
        start = pl.multiple_of(number * 2 * PLANE, LANE)
        cells = orbitals[spin, :, pl.ds(start, 2 * PLANE)].astype(jnp.float32)
        even = pltpu.roll(cells[:, :WIDTH], OFF, 1)
        odd = pltpu.roll(cells[:, 2 * PLANE - WIDTH :], WIDTH - OFF, 1)
        row = spin * EDGE + 2 * number
        for tile in range(TILES):
            span = slice(tile * LANE, (tile + 1) * LANE)
            lines[tile, pl.ds(row, BOX_DEV, stride=ROWS), :] = even[:, span]
            lines[tile, pl.ds(row + 1, BOX_DEV, stride=ROWS), :] = odd[:, span]
        return carry

    lax.fori_loop(0, EDGE // 2, pair, 0, unroll=4)


def gather_tiles(lines, boxes):
    for box in range(BOX_DEV):
        for tile in range(TILES):
            value = lines[tile, box * ROWS : (box + 1) * ROWS, :]
            boxes[box * SPREAD + EMPTY + tile] = value.astype(jnp.bfloat16)


def shift_pair(boxes, moved, density, cells, center, partner, delta, pair_row):
    flat = MARGIN - (delta[1] * EDGE + delta[2])
    column = flat // LANE
    turn = flat - column * LANE
    keep = lax.broadcasted_iota(jnp.int32, (ROWS, LANE), 1) < LANE - turn
    row = lax.broadcasted_iota(jnp.int32, (ROWS, ROWS), 0)
    source = lax.broadcasted_iota(jnp.int32, (ROWS, ROWS), 1)
    same = (row >= EDGE) == (source >= EDGE)
    shifter = (same & (source == row - delta[0])).astype(jnp.float32).astype(jnp.bfloat16)
    first_tile = partner * SPREAD + column
    wide = jnp.concatenate([boxes[first_tile + tile] for tile in range(TILES + 1)], axis=1)
    wide = jnp.dot(shifter, wide, preferred_element_type=jnp.float32)
    turned = [
        pltpu.roll(wide[:, tile * LANE : (tile + 1) * LANE], LANE - turn, 1)
        for tile in range(TILES + 1)
    ]
    for tile in range(TILES):
        span = slice(tile * LANE, (tile + 1) * LANE)
        second = cells[0:1, span] - delta[1]
        third = cells[1:2, span] - delta[2]
        inside = (second >= 0) & (second < EDGE) & (third >= 0) & (third < EDGE)
        inside = inside & (cells[0:1, span] >= 0)
        value = jnp.where(inside, jnp.where(keep, turned[tile], turned[tile + 1]), 0.0)
        product = boxes[center * SPREAD + EMPTY + tile].astype(jnp.float32) * value
        moved[pair_row : pair_row + ROWS, span] = value
        density[pair_row : pair_row + ROWS, span] = product.astype(jnp.bfloat16)


def mirrored(value):
    lanes = LANE - 1 - lax.broadcasted_iota(jnp.int32, value.shape, 1)
    return jnp.take_along_axis(value, lanes, axis=1)


def tile_of(value, tile):
    return value[:, tile * LANE : (tile + 1) * LANE]


def solve(density, work, folded, modes, first, both, inverse, low):
    rows = slice(low, low + 2 * ROWS)
    value = jnp.dot(first[...], density[rows, :], preferred_element_type=jnp.float32)
    for tile in range(FOLDED):
        here = tile_of(value, tile)
        there = mirrored(tile_of(value, TILES - 1 - tile))
        span = slice(tile * LANE, (tile + 1) * LANE)
        folded[0, rows, span] = (here + there).astype(jnp.bfloat16)
        folded[1, rows, span] = (here - there).astype(jnp.bfloat16)
    middle = tile_of(value, FOLDED).astype(jnp.bfloat16)
    for parity in range(2):
        folded[parity, rows, FOLDED * LANE :] = middle
    for parity in range(2):
        for start in range(0, HALF, 256):
            stop = min(start + 256, HALF)
            table = both[2 * parity * HALF : (2 * parity + 1) * HALF, start:stop]
            out = jnp.dot(folded[parity, rows, :], table, preferred_element_type=jnp.float32)
            scale = inverse[:, parity * HALF + start : parity * HALF + stop]
            out = out * jnp.concatenate([scale, scale], axis=0)
            modes[parity, rows, start:stop] = out.astype(jnp.bfloat16)
    for start in range(0, HALF, 256):
        stop = min(start + 256, HALF)
        even, odd = (
            jnp.dot(
                modes[parity, rows, :],
                both[(2 * parity + 1) * HALF : (2 * parity + 2) * HALF, start:stop],
                preferred_element_type=jnp.float32,
            )
            for parity in range(2)
        )
        work[rows, start:stop] = (even + odd).astype(jnp.bfloat16)
        for tile in range(start // LANE, min(stop // LANE, FOLDED)):
            inside = slice(tile * LANE - start, (tile + 1) * LANE - start)
            mirror = mirrored(even[:, inside] - odd[:, inside]).astype(jnp.bfloat16)
            target = TILES - 1 - tile
            work[rows, target * LANE : (target + 1) * LANE] = mirror


def flatten_rows(lines, place):
    half = EDGE // 2
    lanes = lax.broadcasted_iota(jnp.int32, (half, LANE), 1)
    for spin in range(SPINS):
        even = [
            pltpu.roll(lines[tile, pl.ds(spin * EDGE, half, stride=2), :], LANE - OFF, 1)
            for tile in range(TILES)
        ]
        odd = [
            pltpu.roll(lines[tile, pl.ds(spin * EDGE + 1, half, stride=2), :], OFF, 1)
            for tile in range(TILES)
        ]
        for tile in range(TILES - 1):
            place(2 * tile + spin, jnp.where(lanes < LANE - OFF, even[tile], even[tile + 1]))
        place(2 * (TILES - 1) + spin, jnp.where(lanes < LANE // 2, even[TILES - 1], odd[0]))
        for tile in range(1, TILES):
            place(
                2 * (TILES - 1 + tile) + spin,
                jnp.where(lanes < OFF, odd[tile - 1], odd[tile]),
            )


def tile_spins(flat, ready):
    def group(number, carry):
        row = number * 2 * GROUP
        column = number * GROUP * LANE
        for tile in range(GROUP):
            start = pl.multiple_of(column + tile * LANE, LANE)
            ready[:, pl.ds(start, LANE)] = flat[pl.ds(row + 2 * tile, SPINS), :]
        return carry

    lax.fori_loop(0, CELLS // (GROUP * LANE), group, 0)


def mesh_place(device):
    gz = lax.axis_size(AXES[2])
    gy = lax.axis_size(AXES[1])
    return (device // (gy * gz), (device // gz) % gy, device % gz)


def solve_kernel(
    dest_hbm, partners_hbm, anchors_hbm, orbitals_hbm, first_hbm, both_hbm, inverse_hbm, cells_hbm,
    ready,
    dest, partners, anchors, orbitals, first, inverse, cells,
    boxes, moved, density, work, folded, modes, both, lines, flat, box_out, box_in, sends, arrived,
    load_sems, box_send, box_recv, move_send, move_recv,
):
    device = device_number()
    has_next = device < DEVICES - 1
    has_prev = device > 0
    following = mesh_place(jnp.minimum(device + 1, DEVICES - 1))
    previous = mesh_place(jnp.maximum(device - 1, 0))
    barrier = pltpu.get_barrier_semaphore()

    @pl.when(has_next)
    def _():
        pl.semaphore_signal(barrier, inc=1, device_id=following, device_id_type=MESH)

    @pl.when(has_prev)
    def _():
        pl.semaphore_signal(barrier, inc=1, device_id=previous, device_id_type=MESH)

    loads = [
        pltpu.make_async_copy(source, target, load_sems.at[number])
        for number, (source, target) in enumerate(
            (
                (orbitals_hbm.at[0], orbitals.at[0]),
                (orbitals_hbm.at[1], orbitals.at[1]),
                (dest_hbm, dest),
                (partners_hbm, partners),
                (anchors_hbm, anchors),
                (first_hbm, first),
                (cells_hbm, cells),
                (inverse_hbm, inverse),
                (both_hbm, both),
            )
        )
    ]
    for load in loads[:5]:
        load.start()

    def box_copy(way):
        return pltpu.make_async_remote_copy(
            src_ref=box_out.at[way], dst_ref=box_in.at[way],
            send_sem=box_send.at[way], recv_sem=box_recv.at[way],
            device_id=(following, previous)[way], device_id_type=MESH,
        )

    def move_copy(spot):
        return pltpu.make_async_remote_copy(
            src_ref=sends.at[spot], dst_ref=arrived.at[spot],
            send_sem=move_send.at[spot], recv_sem=move_recv.at[spot],
            device_id=previous if spot < 2 else following, device_id_type=MESH,
        )

    blank = jnp.zeros((ROWS, LANE), jnp.bfloat16)
    for box in range(BOX_DEV + 2):
        for tile in range(EMPTY):
            boxes[box * SPREAD + tile] = blank
            boxes[box * SPREAD + EMPTY + TILES + tile] = blank
    for spin in range(SPINS):
        loads[spin].wait()
        unpack_rows(spin, orbitals, lines)
    for load in loads[5:]:
        load.start()
    gather_tiles(lines, boxes)
    for load in loads[2:5]:
        load.wait()
    for way, other in enumerate((device + 1, device - 1)):
        chosen = shared_box(partners, device, other)
        for tile in range(TILES):
            box_out[way, tile] = boxes[chosen * SPREAD + EMPTY + tile]

    pl.semaphore_wait(barrier, has_next.astype(jnp.int32) + has_prev.astype(jnp.int32))

    @pl.when(has_next)
    def _():
        box_copy(0).start()

    @pl.when(has_prev)
    def _():
        box_copy(1).start()

    order = boxes_by_position(dest, device)
    base = device * BOX_DEV

    @pl.when(has_prev)
    def _():
        box_copy(0).wait_recv()
        for tile in range(TILES):
            boxes[BOX_DEV * SPREAD + EMPTY + tile] = box_in[0, tile]

    @pl.when(has_next)
    def _():
        box_copy(1).wait_recv()
        for tile in range(TILES):
            boxes[(BOX_DEV + 1) * SPREAD + EMPTY + tile] = box_in[1, tile]

    def shift_box(spot):
        box = base + order[spot]
        for which in range(2):
            partner = partners[which, box]
            local = partner - base
            place = jnp.where(local < 0, 4, jnp.where(local >= BOX_DEV, 5, local))
            delta = [
                wrapped(anchors[dim, partner] - anchors[dim, box], GRID[dim]) for dim in range(3)
            ]
            row = (spot * 2 + which) * ROWS
            shift_pair(boxes, moved, density, cells, order[spot], place, delta, row)

    for load in loads[5:]:
        load.wait()
    shift_box(TURNS[0])
    for turn, spot in enumerate(TURNS):
        if turn + 1 < BOX_DEV:
            shift_box(TURNS[turn + 1])
        solve(density, work, folded, modes, first, both, inverse, spot * 2 * ROWS)
        span = slice(spot * 2 * ROWS, (spot + 1) * 2 * ROWS)
        potential = jnp.dot(first[...], work[span, :], preferred_element_type=jnp.float32)
        terms = potential * moved[span, :]
        total = terms[:ROWS] + terms[ROWS:]
        for tile in range(TILES):
            lines[tile, :ROWS, :] = total[:, tile * LANE : (tile + 1) * LANE]

        def place(row, value):
            flat[spot, pl.ds(row, EDGE // 2, stride=2 * (2 * TILES - 1)), :] = value

        flatten_rows(lines, place)
        if spot < 3:
            sends[spot] = flat[spot].astype(jnp.bfloat16)

            @pl.when(has_prev if spot < 2 else has_next)
            def _():
                move_copy(spot).start()

    for spot in range(BOX_DEV):
        tile_spins(flat.at[spot], ready.at[spot])
    for spot in (0, 2, 1):
        comes = has_next if spot < 2 else has_prev

        @pl.when(comes)
        def _():
            move_copy(spot).wait_recv()
            flat[spot] = arrived[spot].astype(jnp.float32)
            tile_spins(flat.at[spot], ready.at[BOX_DEV + spot])

    @pl.when(has_next)
    def _():
        box_copy(0).wait_send()
        move_copy(2).wait_send()

    @pl.when(has_prev)
    def _():
        box_copy(1).wait_send()
        move_copy(0).wait_send()
        move_copy(1).wait_send()


def assemble_kernel(dest, ready, out, blank, sems):
    device = device_number()
    blank[...] = jnp.zeros(blank.shape, jnp.float32)
    for slot, source in enumerate(slot_sources(dest, device)):

        @pl.when(source < CAP)
        def _():
            where = jnp.minimum(source, CAP - 1)
            pltpu.make_async_copy(ready.at[where], out.at[slot], sems.at[slot]).start()

        @pl.when(source == CAP)
        def _():
            pltpu.make_async_copy(blank, out.at[slot], sems.at[slot]).start()

    for slot in range(CAP):
        pltpu.make_async_copy(blank, out.at[slot], sems.at[slot]).wait()


VMEM_LIMIT = 42 * 1024 * 1024


def shards(orbitals, dest, partners, anchors):
    first, both, inverse, cells = (jnp.asarray(table) for table in tables())
    operands = (dest, partners.T, anchors.T, orbitals, first, both, inverse, cells)
    operands = [pltpu.with_memory_space_constraint(operand, pltpu.HBM) for operand in operands]
    smem = pl.BlockSpec(memory_space=pltpu.SMEM)
    vmem = pl.BlockSpec(memory_space=pltpu.VMEM)
    hbm = pl.BlockSpec(memory_space=pl.ANY)
    ready = pl.pallas_call(
        solve_kernel,
        out_shape=jax.ShapeDtypeStruct((CAP, SPINS, CELLS), jnp.float32),
        in_specs=[pl.BlockSpec(memory_space=pltpu.HBM)] * 8,
        out_specs=vmem,
        scratch_shapes=[
            pltpu.SMEM((BOXES,), jnp.int32),
            pltpu.SMEM((2, BOXES), jnp.int32),
            pltpu.SMEM((3, BOXES), jnp.int32),
            pltpu.VMEM((SPINS, BOX_DEV, CELLS), jnp.bfloat16),
            pltpu.VMEM(first.shape, first.dtype),
            pltpu.VMEM(inverse.shape, inverse.dtype),
            pltpu.VMEM(cells.shape, cells.dtype),
            pltpu.VMEM(((BOX_DEV + 2) * SPREAD, ROWS, LANE), jnp.bfloat16),
            pltpu.VMEM((PAIR_ROWS, WIDTH), jnp.float32),
            pltpu.VMEM((PAIR_ROWS, WIDTH), jnp.bfloat16),
            pltpu.VMEM((PAIR_ROWS, WIDTH), jnp.bfloat16),
            pltpu.VMEM((2, PAIR_ROWS, HALF), jnp.bfloat16),
            pltpu.VMEM((2, PAIR_ROWS, HALF), jnp.bfloat16),
            pltpu.VMEM(both.shape, both.dtype),
            pltpu.VMEM((TILES, BOX_DEV * ROWS, LANE), jnp.float32),
            pltpu.VMEM((BOX_DEV, OUT_ROWS, LANE), jnp.float32),
            pltpu.VMEM((2, TILES, ROWS, LANE), jnp.bfloat16),
            pltpu.VMEM((2, TILES, ROWS, LANE), jnp.bfloat16),
            pltpu.VMEM((3, OUT_ROWS, LANE), jnp.bfloat16),
            pltpu.VMEM((3, OUT_ROWS, LANE), jnp.bfloat16),
            pltpu.SemaphoreType.DMA((9,)),
            pltpu.SemaphoreType.DMA((2,)),
            pltpu.SemaphoreType.DMA((2,)),
            pltpu.SemaphoreType.DMA((3,)),
            pltpu.SemaphoreType.DMA((3,)),
        ],
        compiler_params=pltpu.CompilerParams(
            vmem_limit_bytes=VMEM_LIMIT, collective_id=0, has_side_effects=True
        ),
    )(*operands)
    out = pl.pallas_call(
        assemble_kernel,
        out_shape=jax.ShapeDtypeStruct((CAP, SPINS, CELLS), jnp.float32),
        in_specs=[smem, hbm],
        out_specs=hbm,
        scratch_shapes=[
            pltpu.VMEM((SPINS, CELLS), jnp.float32),
            pltpu.SemaphoreType.DMA((CAP,)),
        ],
        compiler_params=pltpu.CompilerParams(vmem_limit_bytes=2 * 1024 * 1024),
    )(dest, ready)
    return jnp.transpose(out, (1, 0, 2))


def solution(mesh):
    return jax.shard_map(
        shards,
        mesh=mesh,
        in_specs=(P(None, AXES, None), P(), P(), P()),
        out_specs=P(None, AXES, None),
        check_vma=False,
    )
```

```python
import functools

import jax
import jax.numpy as jnp
import ml_dtypes
import numpy as np
from jax import lax
from jax.experimental import pallas as pl
from jax.experimental.pallas import tpu as pltpu
from jax.sharding import PartitionSpec as P

AXES = ("gx", "gy", "gz")
DEVICES = 128
BOXES = 512
SPINS = 2
EDGE = 40
PLANE = EDGE * EDGE
CELLS = EDGE * PLANE
GRID = (768, 384, 384)
BOX_DEV = 4
CAP = 7
SCREEN = 0.001

LANE = 128
TILES = 13
WIDTH = TILES * LANE
FOLDED = TILES // 2
HALF = (FOLDED + 1) * LANE
OFF = (WIDTH - PLANE) // 2
MARGIN = 7 * LANE
WIDE = WIDTH + 2 * MARGIN
ROWS = SPINS * EDGE
PAIR_ROWS = BOX_DEV * 2 * ROWS
OUT_ROWS = SPINS * CELLS // LANE
GROUP = 25
EARLY = 24
PARTS = ((0, EARLY), (EARLY, EDGE))
SPLIT = SPINS * EARLY
TURNS = (0, 2, 1, 3)
EMPTY = MARGIN // LANE
SPREAD = WIDE // LANE
MESH = pl.DeviceIdType.MESH


def row_order():
    pairs = [(spin, a) for low, high in PARTS for spin in range(SPINS) for a in range(low, high)]
    return tuple(np.array(column) for column in zip(*pairs))


def tables():
    counter = np.arange(EDGE, dtype=np.float64) + 1.0
    angles = np.pi * counter[:, None] * counter[None, :] / (EDGE + 1.0)
    sine = (np.sqrt(2.0 / (EDGE + 1.0)) * np.sin(angles)).astype(ml_dtypes.bfloat16)
    levels = 2.0 - 2.0 * np.cos(np.pi * counter / (EDGE + 1.0))
    plane = (levels[:, None] + levels[None, :]).reshape(-1)
    inverse = np.zeros((EDGE, WIDTH), np.float32)
    inverse[:, OFF : OFF + PLANE] = 1.0 / (levels[:, None] + plane[None, :] + SCREEN)
    spins, planes = row_order()
    inverse = inverse[planes]
    sine32 = sine.astype(np.float32)
    first = sine32[planes][:, planes] * (spins[:, None] == spins[None, :])
    first = np.kron(np.eye(2, dtype=np.float32), first).astype(ml_dtypes.bfloat16)
    steps = np.where(spins[:, None] == spins[None, :], planes[None, :] - planes[:, None], 1000)
    steps = steps.astype(np.int32)
    plane_sine = np.zeros((WIDTH, PLANE), np.float32)
    plane_sine[OFF : OFF + PLANE] = np.kron(sine32, sine32)
    mode = np.arange(PLANE)
    odd = (mode // EDGE + mode % EDGE) % 2
    both = np.zeros((2, 2, HALF, HALF), np.float32)
    scale = np.zeros((2 * EDGE, 2 * HALF), np.float32)
    for parity in range(2):
        chosen = mode[odd == parity]
        both[parity, 0, :, : chosen.size] = plane_sine[:HALF, chosen]
        both[parity, 1] = both[parity, 0].T
        scale[:, parity * HALF : parity * HALF + chosen.size] = inverse[:, OFF + chosen]
    inverse = scale
    both = both.reshape(4 * HALF, HALF).astype(ml_dtypes.bfloat16)
    cells = np.full((2, WIDTH), -1000, np.int32)
    cells[0, OFF : OFF + PLANE] = np.arange(PLANE) // EDGE
    cells[1, OFF : OFF + PLANE] = np.arange(PLANE) % EDGE
    return first, both, inverse, cells, steps


def device_number():
    index = lax.axis_index(AXES[0])
    for name in AXES[1:]:
        index = index * lax.axis_size(name) + lax.axis_index(name)
    return index


def count(dest, first_box, device):
    total = 0
    for number in range(BOX_DEV):
        total = total + (dest[first_box + number] == device).astype(jnp.int32)
    return total


def position(backs, aheads, rank):
    place = backs + rank
    return place + jnp.where((place >= 2) & (aheads > 0), 1, 0)


def boxes_by_position(dest, device):
    base = device * BOX_DEV
    backs = count(dest, base, device - 1)
    aheads = count(dest, base, device + 1)
    order = [0] * BOX_DEV
    back_rank = stay_rank = 0
    for number in range(BOX_DEV):
        goal = dest[base + number]
        back = goal < device
        ahead = goal > device
        place = jnp.where(back, back_rank, jnp.where(ahead, 2, position(backs, aheads, stay_rank)))
        back_rank = back_rank + back.astype(jnp.int32)
        stay_rank = stay_rank + (goal == device).astype(jnp.int32)
        for spot in range(BOX_DEV):
            order[spot] = order[spot] + jnp.where(place == spot, number, 0)
    return order


def slot_sources(dest, device):
    base = device * BOX_DEV
    last = DEVICES - 1
    backs = count(dest, base, device - 1)
    aheads = count(dest, base, device + 1)
    stays = BOX_DEV - backs - aheads
    behind = jnp.maximum(device - 1, 0) * BOX_DEV
    front = jnp.minimum(device + 1, last) * BOX_DEV
    from_prev = jnp.where(device > 0, count(dest, behind, device), 0)
    from_next = jnp.where(device < last, count(dest, front, device), 0)
    sources = []
    for slot in range(CAP):
        rank = slot - from_prev
        late = rank - stays
        sources.append(
            jnp.where(
                rank < 0,
                6,
                jnp.where(
                    late < 0,
                    position(backs, aheads, rank),
                    jnp.where(late < from_next, 4 + late, 7),
                ),
            )
        )
    return sources


def shared_box(partners, device, other):
    inside = jnp.clip(other, 0, DEVICES - 1) * BOX_DEV
    chosen = 0
    for number in range(BOX_DEV):
        for which in range(2):
            partner = partners[which, inside + number] - device * BOX_DEV
            chosen = jnp.where((partner >= 0) & (partner < BOX_DEV), partner, chosen)
    return chosen


def wrapped(difference, extent):
    half = difference + extent // 2
    half = jnp.where(half < 0, half + extent, half)
    half = jnp.where(half >= extent, half - extent, half)
    return half - extent // 2


def pick(values, index):
    chosen = values[0]
    for number in range(1, len(values)):
        chosen = jnp.where(index == number, values[number], chosen)
    return chosen


def unpack_rows(part, orbitals, lines, boxes):
    low, high = PARTS[part]

    def pair(number, carry):
        start = pl.multiple_of(number * 2 * PLANE, LANE)
        for spin in range(SPINS):
            cells = orbitals[spin, :, pl.ds(start, 2 * PLANE)].astype(jnp.float32)
            even = pltpu.roll(cells[:, :WIDTH], OFF, 1)
            odd = pltpu.roll(cells[:, 2 * PLANE - WIDTH :], WIDTH - OFF, 1)
            row = part * SPLIT + spin * (high - low) + 2 * number - low
            for tile in range(TILES):
                span = slice(tile * LANE, (tile + 1) * LANE)
                lines[tile, pl.ds(row, BOX_DEV, stride=ROWS), :] = even[:, span]
                lines[tile, pl.ds(row + 1, BOX_DEV, stride=ROWS), :] = odd[:, span]
        return carry

    lax.fori_loop(low // 2, high // 2, pair, 0, unroll=4)
    rows = slice(part * SPLIT, SPLIT if part == 0 else ROWS)
    for box in range(BOX_DEV):
        for tile in range(TILES):
            value = lines[tile, box * ROWS + rows.start : box * ROWS + rows.stop, :]
            boxes[box * SPREAD + EMPTY + tile, rows, :] = value.astype(jnp.bfloat16)


def shift_pair(boxes, moved, density, cells, steps, center, partner, delta, pair_row):
    flat = MARGIN - (delta[1] * EDGE + delta[2])
    column = flat // LANE
    turn = flat - column * LANE
    keep = lax.broadcasted_iota(jnp.int32, (ROWS, LANE), 1) < LANE - turn
    shifter = (steps[...] == -delta[0]).astype(jnp.float32).astype(jnp.bfloat16)
    first_tile = partner * SPREAD + column
    wide = jnp.concatenate([boxes[first_tile + tile] for tile in range(TILES + 1)], axis=1)
    wide = jnp.dot(shifter, wide, preferred_element_type=jnp.float32)
    turned = [
        pltpu.roll(wide[:, tile * LANE : (tile + 1) * LANE], LANE - turn, 1)
        for tile in range(TILES + 1)
    ]
    for tile in range(TILES):
        span = slice(tile * LANE, (tile + 1) * LANE)
        second = cells[0:1, span] - delta[1]
        third = cells[1:2, span] - delta[2]
        inside = (second >= 0) & (second < EDGE) & (third >= 0) & (third < EDGE)
        inside = inside & (cells[0:1, span] >= 0)
        value = jnp.where(inside, jnp.where(keep, turned[tile], turned[tile + 1]), 0.0)
        product = boxes[center * SPREAD + EMPTY + tile].astype(jnp.float32) * value
        moved[pair_row : pair_row + ROWS, span] = value
        density[pair_row : pair_row + ROWS, span] = product.astype(jnp.bfloat16)


def mirrored(value):
    lanes = LANE - 1 - lax.broadcasted_iota(jnp.int32, value.shape, 1)
    return jnp.take_along_axis(value, lanes, axis=1)


def tile_of(value, tile):
    return value[:, tile * LANE : (tile + 1) * LANE]


def solve(density, work, folded, modes, first, both, inverse, low):
    rows = slice(low, low + 2 * ROWS)
    value = jnp.dot(first[...], density[rows, :], preferred_element_type=jnp.float32)
    for tile in range(FOLDED):
        here = tile_of(value, tile)
        there = mirrored(tile_of(value, TILES - 1 - tile))
        span = slice(tile * LANE, (tile + 1) * LANE)
        folded[0, rows, span] = (here + there).astype(jnp.bfloat16)
        folded[1, rows, span] = (here - there).astype(jnp.bfloat16)
    middle = tile_of(value, FOLDED).astype(jnp.bfloat16)
    for parity in range(2):
        folded[parity, rows, FOLDED * LANE :] = middle
    for parity in range(2):
        for start in range(0, HALF, 256):
            stop = min(start + 256, HALF)
            table = both[2 * parity * HALF : (2 * parity + 1) * HALF, start:stop]
            out = jnp.dot(folded[parity, rows, :], table, preferred_element_type=jnp.float32)
            scale = inverse[:, parity * HALF + start : parity * HALF + stop]
            out = out * jnp.concatenate([scale, scale], axis=0)
            modes[parity, rows, start:stop] = out.astype(jnp.bfloat16)
    for start in range(0, HALF, 256):
        stop = min(start + 256, HALF)
        even, odd = (
            jnp.dot(
                modes[parity, rows, :],
                both[(2 * parity + 1) * HALF : (2 * parity + 2) * HALF, start:stop],
                preferred_element_type=jnp.float32,
            )
            for parity in range(2)
        )
        work[rows, start:stop] = (even + odd).astype(jnp.bfloat16)
        for tile in range(start // LANE, min(stop // LANE, FOLDED)):
            inside = slice(tile * LANE - start, (tile + 1) * LANE - start)
            mirror = mirrored(even[:, inside] - odd[:, inside]).astype(jnp.bfloat16)
            target = TILES - 1 - tile
            work[rows, target * LANE : (target + 1) * LANE] = mirror


def flatten_rows(lines, place):
    half = EDGE // 2
    lanes = lax.broadcasted_iota(jnp.int32, (half, LANE), 1)
    for spin in range(SPINS):
        even = [
            pltpu.roll(lines[tile, pl.ds(spin * EDGE, half, stride=2), :], LANE - OFF, 1)
            for tile in range(TILES)
        ]
        odd = [
            pltpu.roll(lines[tile, pl.ds(spin * EDGE + 1, half, stride=2), :], OFF, 1)
            for tile in range(TILES)
        ]
        for tile in range(TILES - 1):
            place(2 * tile + spin, jnp.where(lanes < LANE - OFF, even[tile], even[tile + 1]))
        place(2 * (TILES - 1) + spin, jnp.where(lanes < LANE // 2, even[TILES - 1], odd[0]))
        for tile in range(1, TILES):
            place(
                2 * (TILES - 1 + tile) + spin,
                jnp.where(lanes < OFF, odd[tile - 1], odd[tile]),
            )


def tile_spins(flat, ready):
    def group(number, carry):
        row = number * 2 * GROUP
        column = number * GROUP * LANE
        for tile in range(GROUP):
            start = pl.multiple_of(column + tile * LANE, LANE)
            ready[:, pl.ds(start, LANE)] = flat[pl.ds(row + 2 * tile, SPINS), :]
        return carry

    lax.fori_loop(0, CELLS // (GROUP * LANE), group, 0)


def mesh_place(device):
    gz = lax.axis_size(AXES[2])
    gy = lax.axis_size(AXES[1])
    return (device // (gy * gz), (device // gz) % gy, device % gz)


def solve_kernel(
    dest_hbm, partners_hbm, anchors_hbm, orbitals_hbm, first_hbm, both_hbm, inverse_hbm, cells_hbm,
    steps_hbm,
    ready,
    dest, partners, anchors, orbitals, first, inverse, cells, steps,
    boxes, moved, density, work, folded, modes, both, lines, flat, early_out, late_out, early_in, late_in, sends, arrived,
    load_sems, box_send, box_recv, move_send, move_recv,
):
    device = device_number()
    has_next = device < DEVICES - 1
    has_prev = device > 0
    following = mesh_place(jnp.minimum(device + 1, DEVICES - 1))
    previous = mesh_place(jnp.maximum(device - 1, 0))
    barrier = pltpu.get_barrier_semaphore()

    @pl.when(has_next)
    def _():
        pl.semaphore_signal(barrier, inc=1, device_id=following, device_id_type=MESH)

    @pl.when(has_prev)
    def _():
        pl.semaphore_signal(barrier, inc=1, device_id=previous, device_id_type=MESH)

    loads = [
        pltpu.make_async_copy(source, target, load_sems.at[number])
        for number, (source, target) in enumerate(
            (
                (orbitals_hbm.at[:, :, : EARLY * PLANE], orbitals.at[:, :, : EARLY * PLANE]),
                (orbitals_hbm.at[:, :, EARLY * PLANE :], orbitals.at[:, :, EARLY * PLANE :]),
                (dest_hbm, dest),
                (partners_hbm, partners),
                (anchors_hbm, anchors),
                (first_hbm, first),
                (cells_hbm, cells),
                (steps_hbm, steps),
                (inverse_hbm, inverse),
                (both_hbm, both),
            )
        )
    ]
    for load in loads[:5]:
        load.start()

    box_out = (early_out, late_out)
    box_in = (early_in, late_in)

    def box_copy(way, part):
        return pltpu.make_async_remote_copy(
            src_ref=box_out[part].at[way], dst_ref=box_in[part].at[way],
            send_sem=box_send.at[2 * part + way], recv_sem=box_recv.at[2 * part + way],
            device_id=(following, previous)[way], device_id_type=MESH,
        )

    def move_copy(spot):
        return pltpu.make_async_remote_copy(
            src_ref=sends.at[spot], dst_ref=arrived.at[spot],
            send_sem=move_send.at[spot], recv_sem=move_recv.at[spot],
            device_id=previous if spot < 2 else following, device_id_type=MESH,
        )

    blank = jnp.zeros((ROWS, LANE), jnp.bfloat16)
    for box in range(BOX_DEV + 2):
        for tile in range(EMPTY):
            boxes[box * SPREAD + tile] = blank
            boxes[box * SPREAD + EMPTY + TILES + tile] = blank
    for part in range(2):
        rows = slice(part * SPLIT, SPLIT if part == 0 else ROWS)
        loads[part].wait()
        unpack_rows(part, orbitals, lines, boxes)
        if part == 0:
            for load in loads[2:5]:
                load.wait()
            for load in loads[5:]:
                load.start()
            chosen = [shared_box(partners, device, other) for other in (device + 1, device - 1)]
        for way in range(2):
            for tile in range(TILES):
                box_out[part][way, tile] = boxes[chosen[way] * SPREAD + EMPTY + tile][rows, :]
        if part == 0:
            pl.semaphore_wait(barrier, has_next.astype(jnp.int32) + has_prev.astype(jnp.int32))

        @pl.when(has_next)
        def _():
            box_copy(0, part).start()

        @pl.when(has_prev)
        def _():
            box_copy(1, part).start()

    order = boxes_by_position(dest, device)
    base = device * BOX_DEV
    for way, comes in ((0, has_prev), (1, has_next)):

        @pl.when(comes)
        def _():
            for part in range(2):
                rows = slice(part * SPLIT, SPLIT if part == 0 else ROWS)
                box_copy(way, part).wait_recv()
                for tile in range(TILES):
                    place = (BOX_DEV + way) * SPREAD + EMPTY + tile
                    boxes[place, rows, :] = box_in[part][way, tile]

    def shift_box(spot):
        box = base + order[spot]
        for which in range(2):
            partner = partners[which, box]
            local = partner - base
            place = jnp.where(local < 0, 4, jnp.where(local >= BOX_DEV, 5, local))
            delta = [
                wrapped(anchors[dim, partner] - anchors[dim, box], GRID[dim]) for dim in range(3)
            ]
            row = (spot * 2 + which) * ROWS
            shift_pair(boxes, moved, density, cells, steps, order[spot], place, delta, row)

    for load in loads[5:]:
        load.wait()
    shift_box(TURNS[0])
    for turn, spot in enumerate(TURNS):
        if turn + 1 < BOX_DEV:
            shift_box(TURNS[turn + 1])
        solve(density, work, folded, modes, first, both, inverse, spot * 2 * ROWS)
        span = slice(spot * 2 * ROWS, (spot + 1) * 2 * ROWS)
        potential = jnp.dot(first[...], work[span, :], preferred_element_type=jnp.float32)
        terms = potential * moved[span, :]
        total = terms[:ROWS] + terms[ROWS:]
        for tile in range(TILES):
            row = 0
            for low, high in PARTS:
                for spin in range(SPINS):
                    piece = total[row : row + high - low, tile * LANE : (tile + 1) * LANE]
                    lines[tile, spin * EDGE + low : spin * EDGE + high, :] = piece
                    row += high - low

        def place(row, value):
            flat[spot, pl.ds(row, EDGE // 2, stride=2 * (2 * TILES - 1)), :] = value

        flatten_rows(lines, place)
        if spot < 3:
            sends[spot] = flat[spot].astype(jnp.bfloat16)

            @pl.when(has_prev if spot < 2 else has_next)
            def _():
                move_copy(spot).start()

    for spot in range(BOX_DEV):
        tile_spins(flat.at[spot], ready.at[spot])
    for spot in (0, 2, 1):
        comes = has_next if spot < 2 else has_prev

        @pl.when(comes)
        def _():
            move_copy(spot).wait_recv()
            flat[spot] = arrived[spot].astype(jnp.float32)
            tile_spins(flat.at[spot], ready.at[BOX_DEV + spot])

    @pl.when(has_next)
    def _():
        box_copy(0, 0).wait_send()
        box_copy(0, 1).wait_send()
        move_copy(2).wait_send()

    @pl.when(has_prev)
    def _():
        box_copy(1, 0).wait_send()
        box_copy(1, 1).wait_send()
        move_copy(0).wait_send()
        move_copy(1).wait_send()


def assemble_kernel(dest, ready, out, blank, sems):
    device = device_number()
    blank[...] = jnp.zeros(blank.shape, jnp.float32)
    for slot, source in enumerate(slot_sources(dest, device)):

        @pl.when(source < CAP)
        def _():
            where = jnp.minimum(source, CAP - 1)
            pltpu.make_async_copy(ready.at[where], out.at[slot], sems.at[slot]).start()

        @pl.when(source == CAP)
        def _():
            pltpu.make_async_copy(blank, out.at[slot], sems.at[slot]).start()

    for slot in range(CAP):
        pltpu.make_async_copy(blank, out.at[slot], sems.at[slot]).wait()


VMEM_LIMIT = 42 * 1024 * 1024


def shards(orbitals, dest, partners, anchors):
    first, both, inverse, cells, steps = (jnp.asarray(table) for table in tables())
    operands = (dest, partners.T, anchors.T, orbitals, first, both, inverse, cells, steps)
    operands = [pltpu.with_memory_space_constraint(operand, pltpu.HBM) for operand in operands]
    smem = pl.BlockSpec(memory_space=pltpu.SMEM)
    vmem = pl.BlockSpec(memory_space=pltpu.VMEM)
    hbm = pl.BlockSpec(memory_space=pl.ANY)
    ready = pl.pallas_call(
        solve_kernel,
        out_shape=jax.ShapeDtypeStruct((CAP, SPINS, CELLS), jnp.float32),
        in_specs=[pl.BlockSpec(memory_space=pltpu.HBM)] * 9,
        out_specs=vmem,
        scratch_shapes=[
            pltpu.SMEM((BOXES,), jnp.int32),
            pltpu.SMEM((2, BOXES), jnp.int32),
            pltpu.SMEM((3, BOXES), jnp.int32),
            pltpu.VMEM((SPINS, BOX_DEV, CELLS), jnp.bfloat16),
            pltpu.VMEM(first.shape, first.dtype),
            pltpu.VMEM(inverse.shape, inverse.dtype),
            pltpu.VMEM(cells.shape, cells.dtype),
            pltpu.VMEM(steps.shape, steps.dtype),
            pltpu.VMEM(((BOX_DEV + 2) * SPREAD, ROWS, LANE), jnp.bfloat16),
            pltpu.VMEM((PAIR_ROWS, WIDTH), jnp.float32),
            pltpu.VMEM((PAIR_ROWS, WIDTH), jnp.bfloat16),
            pltpu.VMEM((PAIR_ROWS, WIDTH), jnp.bfloat16),
            pltpu.VMEM((2, PAIR_ROWS, HALF), jnp.bfloat16),
            pltpu.VMEM((2, PAIR_ROWS, HALF), jnp.bfloat16),
            pltpu.VMEM(both.shape, both.dtype),
            pltpu.VMEM((TILES, BOX_DEV * ROWS, LANE), jnp.float32),
            pltpu.VMEM((BOX_DEV, OUT_ROWS, LANE), jnp.float32),
            pltpu.VMEM((2, TILES, SPLIT, LANE), jnp.bfloat16),
            pltpu.VMEM((2, TILES, ROWS - SPLIT, LANE), jnp.bfloat16),
            pltpu.VMEM((2, TILES, SPLIT, LANE), jnp.bfloat16),
            pltpu.VMEM((2, TILES, ROWS - SPLIT, LANE), jnp.bfloat16),
            pltpu.VMEM((3, OUT_ROWS, LANE), jnp.bfloat16),
            pltpu.VMEM((3, OUT_ROWS, LANE), jnp.bfloat16),
            pltpu.SemaphoreType.DMA((10,)),
            pltpu.SemaphoreType.DMA((4,)),
            pltpu.SemaphoreType.DMA((4,)),
            pltpu.SemaphoreType.DMA((3,)),
            pltpu.SemaphoreType.DMA((3,)),
        ],
        compiler_params=pltpu.CompilerParams(
            vmem_limit_bytes=VMEM_LIMIT, collective_id=0, has_side_effects=True
        ),
    )(*operands)
    out = pl.pallas_call(
        assemble_kernel,
        out_shape=jax.ShapeDtypeStruct((CAP, SPINS, CELLS), jnp.float32),
        in_specs=[smem, hbm],
        out_specs=hbm,
        scratch_shapes=[
            pltpu.VMEM((SPINS, CELLS), jnp.float32),
            pltpu.SemaphoreType.DMA((CAP,)),
        ],
        compiler_params=pltpu.CompilerParams(vmem_limit_bytes=2 * 1024 * 1024),
    )(dest, ready)
    return jnp.transpose(out, (1, 0, 2))


def solution(mesh):
    return jax.shard_map(
        shards,
        mesh=mesh,
        in_specs=(P(None, AXES, None), P(), P(), P()),
        out_specs=P(None, AXES, None),
        check_vma=False,
    )
```

```python
import functools

import jax
import jax.numpy as jnp
import ml_dtypes
import numpy as np
from jax import lax
from jax.experimental import pallas as pl
from jax.experimental.pallas import tpu as pltpu
from jax.sharding import PartitionSpec as P

AXES = ("gx", "gy", "gz")
DEVICES = 128
BOXES = 512
SPINS = 2
EDGE = 40
PLANE = EDGE * EDGE
CELLS = EDGE * PLANE
GRID = (768, 384, 384)
BOX_DEV = 4
CAP = 7
SCREEN = 0.001

LANE = 128
TILES = 13
WIDTH = TILES * LANE
FOLDED = TILES // 2
HALF = (FOLDED + 1) * LANE
OFF = (WIDTH - PLANE) // 2
MARGIN = 7 * LANE
WIDE = WIDTH + 2 * MARGIN
ROWS = SPINS * EDGE
PAIR_ROWS = BOX_DEV * 2 * ROWS
OUT_ROWS = SPINS * CELLS // LANE
GROUP = 25
EARLY = 16
PARTS = ((0, EARLY), (EARLY, EDGE))
SPLIT = SPINS * EARLY
TURNS = (0, 2, 1, 3)
EMPTY = MARGIN // LANE
SPREAD = WIDE // LANE
MESH = pl.DeviceIdType.MESH


def row_order():
    pairs = [(spin, a) for low, high in PARTS for spin in range(SPINS) for a in range(low, high)]
    return tuple(np.array(column) for column in zip(*pairs))


def tables():
    counter = np.arange(EDGE, dtype=np.float64) + 1.0
    angles = np.pi * counter[:, None] * counter[None, :] / (EDGE + 1.0)
    sine = (np.sqrt(2.0 / (EDGE + 1.0)) * np.sin(angles)).astype(ml_dtypes.bfloat16)
    levels = 2.0 - 2.0 * np.cos(np.pi * counter / (EDGE + 1.0))
    plane = (levels[:, None] + levels[None, :]).reshape(-1)
    inverse = np.zeros((EDGE, WIDTH), np.float32)
    inverse[:, OFF : OFF + PLANE] = 1.0 / (levels[:, None] + plane[None, :] + SCREEN)
    spins, planes = row_order()
    inverse = inverse[planes]
    sine32 = sine.astype(np.float32)
    first = sine32[planes][:, planes] * (spins[:, None] == spins[None, :])
    first = np.kron(np.eye(2, dtype=np.float32), first).astype(ml_dtypes.bfloat16)
    steps = np.where(spins[:, None] == spins[None, :], planes[None, :] - planes[:, None], 1000)
    steps = steps.astype(np.int32)
    plane_sine = np.zeros((WIDTH, PLANE), np.float32)
    plane_sine[OFF : OFF + PLANE] = np.kron(sine32, sine32)
    mode = np.arange(PLANE)
    odd = (mode // EDGE + mode % EDGE) % 2
    both = np.zeros((2, 2, HALF, HALF), np.float32)
    scale = np.zeros((2 * EDGE, 2 * HALF), np.float32)
    for parity in range(2):
        chosen = mode[odd == parity]
        both[parity, 0, :, : chosen.size] = plane_sine[:HALF, chosen]
        both[parity, 1] = both[parity, 0].T
        scale[:, parity * HALF : parity * HALF + chosen.size] = inverse[:, OFF + chosen]
    inverse = scale
    both = both.reshape(4 * HALF, HALF).astype(ml_dtypes.bfloat16)
    cells = np.full((2, WIDTH), -1000, np.int32)
    cells[0, OFF : OFF + PLANE] = np.arange(PLANE) // EDGE
    cells[1, OFF : OFF + PLANE] = np.arange(PLANE) % EDGE
    return first, both, inverse, cells, steps


def device_number():
    index = lax.axis_index(AXES[0])
    for name in AXES[1:]:
        index = index * lax.axis_size(name) + lax.axis_index(name)
    return index


def count(dest, first_box, device):
    total = 0
    for number in range(BOX_DEV):
        total = total + (dest[first_box + number] == device).astype(jnp.int32)
    return total


def position(backs, aheads, rank):
    place = backs + rank
    return place + jnp.where((place >= 2) & (aheads > 0), 1, 0)


def boxes_by_position(dest, device):
    base = device * BOX_DEV
    backs = count(dest, base, device - 1)
    aheads = count(dest, base, device + 1)
    order = [0] * BOX_DEV
    back_rank = stay_rank = 0
    for number in range(BOX_DEV):
        goal = dest[base + number]
        back = goal < device
        ahead = goal > device
        place = jnp.where(back, back_rank, jnp.where(ahead, 2, position(backs, aheads, stay_rank)))
        back_rank = back_rank + back.astype(jnp.int32)
        stay_rank = stay_rank + (goal == device).astype(jnp.int32)
        for spot in range(BOX_DEV):
            order[spot] = order[spot] + jnp.where(place == spot, number, 0)
    return order


def slot_sources(dest, device):
    base = device * BOX_DEV
    last = DEVICES - 1
    backs = count(dest, base, device - 1)
    aheads = count(dest, base, device + 1)
    stays = BOX_DEV - backs - aheads
    behind = jnp.maximum(device - 1, 0) * BOX_DEV
    front = jnp.minimum(device + 1, last) * BOX_DEV
    from_prev = jnp.where(device > 0, count(dest, behind, device), 0)
    from_next = jnp.where(device < last, count(dest, front, device), 0)
    sources = []
    for slot in range(CAP):
        rank = slot - from_prev
        late = rank - stays
        sources.append(
            jnp.where(
                rank < 0,
                6,
                jnp.where(
                    late < 0,
                    position(backs, aheads, rank),
                    jnp.where(late < from_next, 4 + late, 7),
                ),
            )
        )
    return sources


def shared_box(partners, device, other):
    inside = jnp.clip(other, 0, DEVICES - 1) * BOX_DEV
    chosen = 0
    for number in range(BOX_DEV):
        for which in range(2):
            partner = partners[which, inside + number] - device * BOX_DEV
            chosen = jnp.where((partner >= 0) & (partner < BOX_DEV), partner, chosen)
    return chosen


def wrapped(difference, extent):
    half = difference + extent // 2
    half = jnp.where(half < 0, half + extent, half)
    half = jnp.where(half >= extent, half - extent, half)
    return half - extent // 2


def pick(values, index):
    chosen = values[0]
    for number in range(1, len(values)):
        chosen = jnp.where(index == number, values[number], chosen)
    return chosen


def unpack_rows(part, orbitals, lines, boxes):
    low, high = PARTS[part]

    def pair(number, carry):
        start = pl.multiple_of(number * 2 * PLANE, LANE)
        for spin in range(SPINS):
            cells = orbitals[spin, :, pl.ds(start, 2 * PLANE)].astype(jnp.float32)
            even = pltpu.roll(cells[:, :WIDTH], OFF, 1)
            odd = pltpu.roll(cells[:, 2 * PLANE - WIDTH :], WIDTH - OFF, 1)
            row = part * SPLIT + spin * (high - low) + 2 * number - low
            for tile in range(TILES):
                span = slice(tile * LANE, (tile + 1) * LANE)
                lines[tile, pl.ds(row, BOX_DEV, stride=ROWS), :] = even[:, span]
                lines[tile, pl.ds(row + 1, BOX_DEV, stride=ROWS), :] = odd[:, span]
        return carry

    lax.fori_loop(low // 2, high // 2, pair, 0, unroll=4)
    rows = slice(part * SPLIT, SPLIT if part == 0 else ROWS)
    for box in range(BOX_DEV):
        for tile in range(TILES):
            value = lines[tile, box * ROWS + rows.start : box * ROWS + rows.stop, :]
            boxes[box * SPREAD + EMPTY + tile, rows, :] = value.astype(jnp.bfloat16)


def shift_pair(boxes, moved, density, cells, steps, center, partner, delta, pair_row):
    flat = MARGIN - (delta[1] * EDGE + delta[2])
    column = flat // LANE
    turn = flat - column * LANE
    keep = lax.broadcasted_iota(jnp.int32, (ROWS, LANE), 1) < LANE - turn
    shifter = (steps[...] == -delta[0]).astype(jnp.float32).astype(jnp.bfloat16)
    first_tile = partner * SPREAD + column
    wide = jnp.concatenate([boxes[first_tile + tile] for tile in range(TILES + 1)], axis=1)
    wide = jnp.dot(shifter, wide, preferred_element_type=jnp.float32)
    turned = [
        pltpu.roll(wide[:, tile * LANE : (tile + 1) * LANE], LANE - turn, 1)
        for tile in range(TILES + 1)
    ]
    for tile in range(TILES):
        span = slice(tile * LANE, (tile + 1) * LANE)
        second = cells[0:1, span] - delta[1]
        third = cells[1:2, span] - delta[2]
        inside = (second >= 0) & (second < EDGE) & (third >= 0) & (third < EDGE)
        inside = inside & (cells[0:1, span] >= 0)
        value = jnp.where(inside, jnp.where(keep, turned[tile], turned[tile + 1]), 0.0)
        product = boxes[center * SPREAD + EMPTY + tile].astype(jnp.float32) * value
        moved[pair_row : pair_row + ROWS, span] = value
        density[pair_row : pair_row + ROWS, span] = product.astype(jnp.bfloat16)


def mirrored(value):
    lanes = LANE - 1 - lax.broadcasted_iota(jnp.int32, value.shape, 1)
    return jnp.take_along_axis(value, lanes, axis=1)


def tile_of(value, tile):
    return value[:, tile * LANE : (tile + 1) * LANE]


def solve(density, work, folded, modes, first, both, inverse, low):
    rows = slice(low, low + 2 * ROWS)
    value = jnp.dot(first[...], density[rows, :], preferred_element_type=jnp.float32)
    for tile in range(FOLDED):
        here = tile_of(value, tile)
        there = mirrored(tile_of(value, TILES - 1 - tile))
        span = slice(tile * LANE, (tile + 1) * LANE)
        folded[0, rows, span] = (here + there).astype(jnp.bfloat16)
        folded[1, rows, span] = (here - there).astype(jnp.bfloat16)
    middle = tile_of(value, FOLDED).astype(jnp.bfloat16)
    for parity in range(2):
        folded[parity, rows, FOLDED * LANE :] = middle
    for parity in range(2):
        for start in range(0, HALF, 256):
            stop = min(start + 256, HALF)
            table = both[2 * parity * HALF : (2 * parity + 1) * HALF, start:stop]
            out = jnp.dot(folded[parity, rows, :], table, preferred_element_type=jnp.float32)
            scale = inverse[:, parity * HALF + start : parity * HALF + stop]
            out = out * jnp.concatenate([scale, scale], axis=0)
            modes[parity, rows, start:stop] = out.astype(jnp.bfloat16)
    for start in range(0, HALF, 256):
        stop = min(start + 256, HALF)
        even, odd = (
            jnp.dot(
                modes[parity, rows, :],
                both[(2 * parity + 1) * HALF : (2 * parity + 2) * HALF, start:stop],
                preferred_element_type=jnp.float32,
            )
            for parity in range(2)
        )
        work[rows, start:stop] = (even + odd).astype(jnp.bfloat16)
        for tile in range(start // LANE, min(stop // LANE, FOLDED)):
            inside = slice(tile * LANE - start, (tile + 1) * LANE - start)
            mirror = mirrored(even[:, inside] - odd[:, inside]).astype(jnp.bfloat16)
            target = TILES - 1 - tile
            work[rows, target * LANE : (target + 1) * LANE] = mirror


def flatten_rows(lines, place):
    half = EDGE // 2
    lanes = lax.broadcasted_iota(jnp.int32, (half, LANE), 1)
    for spin in range(SPINS):
        even = [
            pltpu.roll(lines[tile, pl.ds(spin * EDGE, half, stride=2), :], LANE - OFF, 1)
            for tile in range(TILES)
        ]
        odd = [
            pltpu.roll(lines[tile, pl.ds(spin * EDGE + 1, half, stride=2), :], OFF, 1)
            for tile in range(TILES)
        ]
        for tile in range(TILES - 1):
            place(2 * tile + spin, jnp.where(lanes < LANE - OFF, even[tile], even[tile + 1]))
        place(2 * (TILES - 1) + spin, jnp.where(lanes < LANE // 2, even[TILES - 1], odd[0]))
        for tile in range(1, TILES):
            place(
                2 * (TILES - 1 + tile) + spin,
                jnp.where(lanes < OFF, odd[tile - 1], odd[tile]),
            )


def tile_spins(flat, ready):
    def group(number, carry):
        row = number * 2 * GROUP
        column = number * GROUP * LANE
        for tile in range(GROUP):
            start = pl.multiple_of(column + tile * LANE, LANE)
            ready[:, pl.ds(start, LANE)] = flat[pl.ds(row + 2 * tile, SPINS), :]
        return carry

    lax.fori_loop(0, CELLS // (GROUP * LANE), group, 0)


def mesh_place(device):
    gz = lax.axis_size(AXES[2])
    gy = lax.axis_size(AXES[1])
    return (device // (gy * gz), (device // gz) % gy, device % gz)


def solve_kernel(
    dest_hbm, partners_hbm, anchors_hbm, orbitals_hbm, first_hbm, both_hbm, inverse_hbm, cells_hbm,
    steps_hbm,
    ready,
    dest, partners, anchors, orbitals, first, inverse, cells, steps,
    boxes, moved, density, work, folded, modes, both, lines, flat, early_out, late_out, early_in, late_in, sends, arrived,
    load_sems, box_send, box_recv, move_send, move_recv,
):
    device = device_number()
    has_next = device < DEVICES - 1
    has_prev = device > 0
    following = mesh_place(jnp.minimum(device + 1, DEVICES - 1))
    previous = mesh_place(jnp.maximum(device - 1, 0))
    barrier = pltpu.get_barrier_semaphore()

    @pl.when(has_next)
    def _():
        pl.semaphore_signal(barrier, inc=1, device_id=following, device_id_type=MESH)

    @pl.when(has_prev)
    def _():
        pl.semaphore_signal(barrier, inc=1, device_id=previous, device_id_type=MESH)

    loads = [
        pltpu.make_async_copy(source, target, load_sems.at[number])
        for number, (source, target) in enumerate(
            (
                (orbitals_hbm.at[:, :, : EARLY * PLANE], orbitals.at[:, :, : EARLY * PLANE]),
                (orbitals_hbm.at[:, :, EARLY * PLANE :], orbitals.at[:, :, EARLY * PLANE :]),
                (dest_hbm, dest),
                (partners_hbm, partners),
                (anchors_hbm, anchors),
                (first_hbm, first),
                (cells_hbm, cells),
                (steps_hbm, steps),
                (inverse_hbm, inverse),
                (both_hbm, both),
            )
        )
    ]
    for load in loads[:5]:
        load.start()

    box_out = (early_out, late_out)
    box_in = (early_in, late_in)

    def box_copy(way, part):
        return pltpu.make_async_remote_copy(
            src_ref=box_out[part].at[way], dst_ref=box_in[part].at[way],
            send_sem=box_send.at[2 * part + way], recv_sem=box_recv.at[2 * part + way],
            device_id=(following, previous)[way], device_id_type=MESH,
        )

    def move_copy(spot):
        return pltpu.make_async_remote_copy(
            src_ref=sends.at[spot], dst_ref=arrived.at[spot],
            send_sem=move_send.at[spot], recv_sem=move_recv.at[spot],
            device_id=previous if spot < 2 else following, device_id_type=MESH,
        )

    blank = jnp.zeros((ROWS, LANE), jnp.bfloat16)
    for box in range(BOX_DEV + 2):
        for tile in range(EMPTY):
            boxes[box * SPREAD + tile] = blank
            boxes[box * SPREAD + EMPTY + TILES + tile] = blank
    for part in range(2):
        rows = slice(part * SPLIT, SPLIT if part == 0 else ROWS)
        loads[part].wait()
        unpack_rows(part, orbitals, lines, boxes)
        if part == 0:
            for load in loads[2:5]:
                load.wait()
            for load in loads[5:]:
                load.start()
            chosen = [shared_box(partners, device, other) for other in (device + 1, device - 1)]
        for way in range(2):
            for tile in range(TILES):
                box_out[part][way, tile] = boxes[chosen[way] * SPREAD + EMPTY + tile][rows, :]
        if part == 0:
            pl.semaphore_wait(barrier, has_next.astype(jnp.int32) + has_prev.astype(jnp.int32))

        @pl.when(has_next)
        def _():
            box_copy(0, part).start()

        @pl.when(has_prev)
        def _():
            box_copy(1, part).start()

    order = boxes_by_position(dest, device)
    base = device * BOX_DEV
    for way, comes in ((0, has_prev), (1, has_next)):

        @pl.when(comes)
        def _():
            for part in range(2):
                rows = slice(part * SPLIT, SPLIT if part == 0 else ROWS)
                box_copy(way, part).wait_recv()
                for tile in range(TILES):
                    place = (BOX_DEV + way) * SPREAD + EMPTY + tile
                    boxes[place, rows, :] = box_in[part][way, tile]

    def shift_box(spot):
        box = base + order[spot]
        for which in range(2):
            partner = partners[which, box]
            local = partner - base
            place = jnp.where(local < 0, 4, jnp.where(local >= BOX_DEV, 5, local))
            delta = [
                wrapped(anchors[dim, partner] - anchors[dim, box], GRID[dim]) for dim in range(3)
            ]
            row = (spot * 2 + which) * ROWS
            shift_pair(boxes, moved, density, cells, steps, order[spot], place, delta, row)

    for load in loads[5:]:
        load.wait()
    shift_box(TURNS[0])
    for turn, spot in enumerate(TURNS):
        if turn + 1 < BOX_DEV:
            shift_box(TURNS[turn + 1])
        solve(density, work, folded, modes, first, both, inverse, spot * 2 * ROWS)
        span = slice(spot * 2 * ROWS, (spot + 1) * 2 * ROWS)
        potential = jnp.dot(first[...], work[span, :], preferred_element_type=jnp.float32)
        terms = potential * moved[span, :]
        total = terms[:ROWS] + terms[ROWS:]
        for tile in range(TILES):
            row = 0
            for low, high in PARTS:
                for spin in range(SPINS):
                    piece = total[row : row + high - low, tile * LANE : (tile + 1) * LANE]
                    lines[tile, spin * EDGE + low : spin * EDGE + high, :] = piece
                    row += high - low

        def place(row, value):
            flat[spot, pl.ds(row, EDGE // 2, stride=2 * (2 * TILES - 1)), :] = value

        flatten_rows(lines, place)
        if spot < 3:
            sends[spot] = flat[spot].astype(jnp.bfloat16)

            @pl.when(has_prev if spot < 2 else has_next)
            def _():
                move_copy(spot).start()

    for spot in range(BOX_DEV):
        tile_spins(flat.at[spot], ready.at[spot])
    for spot in (0, 2, 1):
        comes = has_next if spot < 2 else has_prev

        @pl.when(comes)
        def _():
            move_copy(spot).wait_recv()
            flat[spot] = arrived[spot].astype(jnp.float32)
            tile_spins(flat.at[spot], ready.at[BOX_DEV + spot])

    @pl.when(has_next)
    def _():
        box_copy(0, 0).wait_send()
        box_copy(0, 1).wait_send()
        move_copy(2).wait_send()

    @pl.when(has_prev)
    def _():
        box_copy(1, 0).wait_send()
        box_copy(1, 1).wait_send()
        move_copy(0).wait_send()
        move_copy(1).wait_send()


def assemble_kernel(dest, ready, out, blank, sems):
    device = device_number()
    blank[...] = jnp.zeros(blank.shape, jnp.float32)
    for slot, source in enumerate(slot_sources(dest, device)):

        @pl.when(source < CAP)
        def _():
            where = jnp.minimum(source, CAP - 1)
            pltpu.make_async_copy(ready.at[where], out.at[slot], sems.at[slot]).start()

        @pl.when(source == CAP)
        def _():
            pltpu.make_async_copy(blank, out.at[slot], sems.at[slot]).start()

    for slot in range(CAP):
        pltpu.make_async_copy(blank, out.at[slot], sems.at[slot]).wait()


VMEM_LIMIT = 42 * 1024 * 1024


def shards(orbitals, dest, partners, anchors):
    first, both, inverse, cells, steps = (jnp.asarray(table) for table in tables())
    operands = (dest, partners.T, anchors.T, orbitals, first, both, inverse, cells, steps)
    operands = [pltpu.with_memory_space_constraint(operand, pltpu.HBM) for operand in operands]
    smem = pl.BlockSpec(memory_space=pltpu.SMEM)
    vmem = pl.BlockSpec(memory_space=pltpu.VMEM)
    hbm = pl.BlockSpec(memory_space=pl.ANY)
    ready = pl.pallas_call(
        solve_kernel,
        out_shape=jax.ShapeDtypeStruct((CAP, SPINS, CELLS), jnp.float32),
        in_specs=[pl.BlockSpec(memory_space=pltpu.HBM)] * 9,
        out_specs=vmem,
        scratch_shapes=[
            pltpu.SMEM((BOXES,), jnp.int32),
            pltpu.SMEM((2, BOXES), jnp.int32),
            pltpu.SMEM((3, BOXES), jnp.int32),
            pltpu.VMEM((SPINS, BOX_DEV, CELLS), jnp.bfloat16),
            pltpu.VMEM(first.shape, first.dtype),
            pltpu.VMEM(inverse.shape, inverse.dtype),
            pltpu.VMEM(cells.shape, cells.dtype),
            pltpu.VMEM(steps.shape, steps.dtype),
            pltpu.VMEM(((BOX_DEV + 2) * SPREAD, ROWS, LANE), jnp.bfloat16),
            pltpu.VMEM((PAIR_ROWS, WIDTH), jnp.float32),
            pltpu.VMEM((PAIR_ROWS, WIDTH), jnp.bfloat16),
            pltpu.VMEM((PAIR_ROWS, WIDTH), jnp.bfloat16),
            pltpu.VMEM((2, PAIR_ROWS, HALF), jnp.bfloat16),
            pltpu.VMEM((2, PAIR_ROWS, HALF), jnp.bfloat16),
            pltpu.VMEM(both.shape, both.dtype),
            pltpu.VMEM((TILES, BOX_DEV * ROWS, LANE), jnp.float32),
            pltpu.VMEM((BOX_DEV, OUT_ROWS, LANE), jnp.float32),
            pltpu.VMEM((2, TILES, SPLIT, LANE), jnp.bfloat16),
            pltpu.VMEM((2, TILES, ROWS - SPLIT, LANE), jnp.bfloat16),
            pltpu.VMEM((2, TILES, SPLIT, LANE), jnp.bfloat16),
            pltpu.VMEM((2, TILES, ROWS - SPLIT, LANE), jnp.bfloat16),
            pltpu.VMEM((3, OUT_ROWS, LANE), jnp.bfloat16),
            pltpu.VMEM((3, OUT_ROWS, LANE), jnp.bfloat16),
            pltpu.SemaphoreType.DMA((10,)),
            pltpu.SemaphoreType.DMA((4,)),
            pltpu.SemaphoreType.DMA((4,)),
            pltpu.SemaphoreType.DMA((3,)),
            pltpu.SemaphoreType.DMA((3,)),
        ],
        compiler_params=pltpu.CompilerParams(
            vmem_limit_bytes=VMEM_LIMIT, collective_id=0, has_side_effects=True
        ),
    )(*operands)
    out = pl.pallas_call(
        assemble_kernel,
        out_shape=jax.ShapeDtypeStruct((CAP, SPINS, CELLS), jnp.float32),
        in_specs=[smem, hbm],
        out_specs=hbm,
        scratch_shapes=[
            pltpu.VMEM((SPINS, CELLS), jnp.float32),
            pltpu.SemaphoreType.DMA((CAP,)),
        ],
        compiler_params=pltpu.CompilerParams(vmem_limit_bytes=2 * 1024 * 1024),
    )(dest, ready)
    return jnp.transpose(out, (1, 0, 2))


def solution(mesh):
    return jax.shard_map(
        shards,
        mesh=mesh,
        in_specs=(P(None, AXES, None), P(), P(), P()),
        out_specs=P(None, AXES, None),
        check_vma=False,
    )
```
